32 devices in a mesh: morton: 8 (over y, x, core), lane: 4 (over z).
Axes of the slice: x: 2, y: 2, z: 4, core: 2. Of those that a mesh axis runs over, the one named last changes fastest.
Arguments:
- multipoles: bfloat16 [8, 512, 296], P('morton', 'lane'), may hold values from -6 to 6
- counts: int32 [8, 512], P('morton', 'lane'), may hold values from 1 to 12
- sources: int32 [8, 512, 12], P('morton', 'lane'), may hold values from 0 to 1151, as said below
- relpos: int32 [8, 512, 12], P('morton', 'lane'), may hold values from 0 to 11, as said below
- operators: bfloat16 [12, 296, 296], P('lane'), may hold values from -0.375 to 0.375
- c2e: bfloat16 [296, 296], replicated, may hold values from -0.375 to 0.375
Outputs:
- local_density: float32 [8, 512, 296], P('morton', 'lane')
The draws below stay inside these ranges and needn't reach their ends.
Inputs may be any that keep to these rules, and one draw needn't show every extreme that they name: `sources`: every live slot names a source box inside the grid of 8 x 4 devices' boxes. `relpos`: the ids of one box's slots are all different.
All inputs are finite; a program needn't handle non-finite values.
Results may differ from the reference program's by a relative error of at most 0.0029.
Values may be sent and summed in bfloat16 or wider, within the bound.
No kernel may reach another device: no remote copies, remote signals or barrier semaphores. Data moves between devices by JAX's collectives and lax.ppermute only.
A program may use at most 64 MiB of HBM per device.

```python
import jax
import jax.numpy as jnp
from jax import lax

EQ = 296
BOX_DEV = 128
SEGS = 8
LANES = 4
REL = 12


def build_lists(key):
    keys = [jax.random.fold_in(key, 7100 + index) for index in range(8)]
    ndevice = SEGS * LANES
    nboxes = ndevice * BOX_DEV
    slot_ids = jnp.arange(REL, dtype=jnp.int32)
    scores = jax.random.randint(keys[0], (ndevice, REL), 0, 1 << 20) * REL + slot_ids[None, :]
    perm = jnp.argsort(scores, axis=1).astype(jnp.int32)
    active = jax.random.randint(keys[1], (ndevice,), 1, REL + 1)
    active = active.at[0].set(REL)
    owner = jnp.arange(nboxes, dtype=jnp.int32) // BOX_DEV
    box_active = active[owner]
    cnt = jax.random.randint(keys[2], (nboxes,), 0, 1 << 20) % box_active + 1
    cnt = cnt.at[0].set(REL)
    second = jax.random.randint(keys[3], (nboxes, REL), 0, 1 << 20) * REL + slot_ids[None, :]
    second = second + (slot_ids[None, :] >= box_active[:, None]).astype(jnp.int32) * (1 << 26)
    order = jnp.argsort(second, axis=1).astype(jnp.int32)
    rel = jnp.take_along_axis(perm[owner], order, axis=1)
    step_seg = jax.random.randint(keys[4], (nboxes, REL), -1, 2)
    step_lane = jax.random.randint(keys[5], (nboxes, REL), -1, 2)
    segment = (owner // LANES)[:, None]
    subrange = (owner % LANES)[:, None]
    seg_src = jnp.clip(segment + step_seg, 0, SEGS - 1)
    lane_src = jnp.clip(subrange + step_lane, 0, LANES - 1)
    neighbour = (seg_src - segment + 1) * 3 + (lane_src - subrange + 1)
    offset = jax.random.randint(keys[6], (nboxes, REL), 0, BOX_DEV)
    code = (neighbour * BOX_DEV + offset).astype(jnp.int32)
    return (cnt.astype(jnp.int32).reshape(SEGS, LANES * BOX_DEV), code.reshape(SEGS, LANES * BOX_DEV, REL), rel.astype(jnp.int32).reshape(SEGS, LANES * BOX_DEV, REL))


def draw_counts(key, part):
    return build_lists(key)[0]


def draw_sources(key, part):
    return build_lists(key)[1]


def draw_relpos(key, part):
    return build_lists(key)[2]


def level_of(key, shape, shards, smallest, top_value):
    factor_of = 1.0
    for dim, blocks in shards:
        heights = jax.random.uniform(jax.random.fold_in(jax.random.fold_in(key, 6), dim), (blocks,), jnp.float32, smallest / len(shards), top_value / len(shards))
        factor_of = factor_of * jnp.repeat(jnp.exp(heights), shape[dim] // blocks).reshape((-1,) + (1,) * (len(shape) - 1 - dim))
    return factor_of


def scatter_about(key, extent, scale, most, split=(), kind=jnp.bfloat16):
    level = level_of(key, extent, split, -0.22, 0.18) if split else 1.0
    array = jax.random.normal(key, extent, jnp.float32) * scale * level
    return jnp.minimum(jnp.maximum(array, -most), most).astype(kind)


def setup_inputs(seed: int = 0) -> dict:
    key_of = jax.random.split(jax.random.key(seed), 7)
    multipoles = scatter_about(key_of[0], (SEGS, LANES * BOX_DEV, EQ), 1.0, 6.0, ((0, 8), (1, 4)))
    counts = draw_counts(jax.random.fold_in(key_of[6], 71), 0)
    sources = draw_sources(jax.random.fold_in(key_of[6], 71), 0)
    relpos = draw_relpos(jax.random.fold_in(key_of[6], 71), 0)
    operators = scatter_about(key_of[4], (REL, EQ, EQ), EQ ** -0.5, 0.375, ((0, 4),))
    c2e = scatter_about(key_of[5], (EQ, EQ), EQ ** -0.5, 0.375)
    return {"multipoles": multipoles, "counts": counts, "sources": sources, "relpos": relpos, "operators": operators, "c2e": c2e}


def reference(multipoles, counts, sources, relpos, operators, c2e):
    flat = multipoles.reshape(SEGS * LANES * BOX_DEV, EQ)
    cnt = counts.reshape(SEGS * LANES, BOX_DEV)
    codes = sources.reshape(SEGS * LANES, BOX_DEV, REL)
    rel = relpos.reshape(SEGS * LANES, BOX_DEV, REL)
    slots = jnp.arange(REL, dtype=jnp.int32)
    devices = jnp.arange(SEGS * LANES, dtype=jnp.int32)

    def block(items):
        device, count_row, code_row, rel_row = items
        segment = device // LANES
        subrange = device % LANES
        neighbour = code_row // BOX_DEV
        offset = code_row % BOX_DEV
        seg_src = segment + neighbour // 3 - 1
        lane_src = subrange + neighbour % 3 - 1
        global_src = ((seg_src * LANES + lane_src) * BOX_DEV + offset).astype(jnp.int32)
        live = slots[None, :] < count_row[:, None]

        def step(index, total):
            hit = live & (rel_row == index)
            has = jnp.any(hit, axis=1)
            where_src = jnp.sum(jnp.where(hit, global_src, 0), axis=1).astype(jnp.int32)
            rows = jnp.where(has[:, None], flat[where_src], jnp.zeros((), flat.dtype))
            matrix = lax.dynamic_index_in_dim(operators, index, 0, keepdims=False)
            return total + jnp.dot(rows, matrix, preferred_element_type=jnp.float32)

        total = lax.fori_loop(0, REL, step, jnp.zeros((BOX_DEV, EQ), jnp.float32))
        check = total.astype(jnp.bfloat16)
        return jnp.dot(check, c2e, preferred_element_type=jnp.float32)

    result = lax.map(block, (devices, cnt, codes, rel))
    return result.reshape(SEGS, LANES * BOX_DEV, EQ)
```

```python
import functools

import jax
import jax.numpy as jnp
from jax import lax
from jax.experimental import pallas as pl
from jax.experimental.pallas import tpu as pltpu
from jax.sharding import PartitionSpec as P


def cdiv(a, b):
    return -(-a // b)


def pairs_xor(count, mask):
    return [(i, i ^ mask) for i in range(count)]


def pairs_odd(count):
    out = []
    for i in range(1, count - 1, 2):
        out += [(i, i + 1), (i + 1, i)]
    return out


def gather_kernel(boxes, per, lanes, ids, counts, sources, relpos, column, twin, other, out):
    lane_id, seg_id = ids[0], ids[1]
    code = sources[...]
    rel = relpos[...]
    width = out.shape[2]
    slot = lax.broadcasted_iota(jnp.int32, rel.shape, 0)
    live = slot < counts[...]
    nb = jnp.zeros_like(code)
    for k in range(1, 9):
        nb = nb + (code >= k * boxes).astype(jnp.int32)
    a = (nb >= 3).astype(jnp.int32) + (nb >= 6).astype(jnp.int32)
    b = nb - 3 * a
    offset = code - nb * boxes

    def place(v, odd):
        return jnp.where(v == 1, 0, jnp.where(v == 2 - 2 * odd, 1, 2))

    mapped = (place(a, seg_id % 2) * 3 + place(b, lane_id % 2)) * boxes + offset + 1
    mapped = jnp.where(live, mapped, 0)
    rows = []
    for g in range(lanes):
        for i in range(per):
            wanted = (lane_id ^ g) * per + i
            rows.append(jnp.sum(jnp.where(rel == wanted, mapped, 0), axis=0, keepdims=True) - 1)
    fill = jnp.full((boxes - len(rows), boxes), -1, jnp.int32)
    index = jnp.concatenate(rows + [fill], axis=0).T
    parts = []
    for ref in (column, twin, other):
        for j in range(3):
            parts.append(ref[pl.ds(j * width, width), :])
    table = jnp.concatenate(parts, axis=1)
    spot = lax.broadcasted_iota(jnp.int32, (boxes, 9 * boxes), 1)
    for g in range(lanes):
        picks = []
        for i in range(per):
            at = g * per + i
            picks.append((index[:, at : at + 1] == spot).astype(jnp.float32).astype(jnp.bfloat16))
        picks = jnp.concatenate(picks, axis=0)
        found = lax.dot_general(picks, table, (((1,), (1,)), ((), ())), preferred_element_type=jnp.float32)
        out[g * per : (g + 1) * per] = found.astype(jnp.bfloat16).reshape(per, boxes, width)


def starts_of(rows, chunk, index):
    return pl.multiple_of(jnp.minimum(index * chunk, rows - chunk), 8)


def assemble(buffer, chunks, masks, seg_id, rows, chunk):
    for j, mask in enumerate(masks):
        at = starts_of(rows, chunk, seg_id ^ mask)
        buffer[pl.ds(at, chunk), :] = chunks[pl.ds(j * chunk, chunk), :]


def accumulate(total, picked, first, buffer, per, width):
    for i in range(per):
        term = jnp.dot(picked[first + i], buffer[pl.ds(i * width, width), :], preferred_element_type=jnp.float32)
        total = term if total is None else total + term
    return total


def early_kernel(masks, groups, per, width, rows, chunk, ids, picked, own, *refs):
    n = len(groups)
    chunks, out, buffer = refs[:n], refs[n], refs[n + 1]
    total = None
    for i in range(per):
        term = jnp.dot(picked[i], own[i], preferred_element_type=jnp.float32)
        total = term if total is None else total + term
    for k in range(n):
        assemble(buffer.at[k], chunks[k], masks[k], ids[1], rows, chunk)
        total = accumulate(total, picked, groups[k] * per, buffer.at[k], per, width)
    out[...] = total


def late_kernel(masks, groups, per, width, rows, chunk, ids, picked, before, c2e, *refs):
    n = len(groups)
    chunks, out, buffer = refs[:n], refs[n], refs[n + 1]
    total = before[...]
    for k in range(n):
        assemble(buffer.at[k], chunks[k], masks[k], ids[1], rows, chunk)
        total = accumulate(total, picked, groups[k] * per, buffer.at[k], per, width)
    check = total.astype(jnp.bfloat16)
    out[...] = jnp.dot(check, c2e[...], preferred_element_type=jnp.float32).T


def per_device(multipoles, counts, sources, relpos, operators, c2e):
    segs, lanes = lax.axis_size("morton"), lax.axis_size("lane")
    seg_id, lane_id = lax.axis_index("morton"), lax.axis_index("lane")
    boxes, width = multipoles.shape[1:]
    per = operators.shape[0]
    slots = sources.shape[2]
    rows = per * width
    chunk = 8 * cdiv(rows // 8, segs)
    bits = segs.bit_length() - 1
    block = multipoles[0].T
    flat = operators.reshape(rows, width)
    mine = lax.dynamic_slice_in_dim(flat, jnp.minimum(seg_id * chunk, rows - chunk), chunk, 0)
    vec = jnp.stack([lane_id, seg_id]).astype(jnp.int32)

    near = lax.ppermute(block, "lane", pairs_xor(lanes, 1))
    arrived = []
    for k in range(1, lanes):
        arrived.append(lax.ppermute(mine, "lane", pairs_xor(lanes, k)))

    far = lax.ppermute(block, "lane", pairs_odd(lanes))
    column = jnp.concatenate([block, near, far], axis=0)
    twin = lax.ppermute(column, "morton", pairs_xor(segs, 1))
    other = lax.ppermute(column, "morton", pairs_odd(segs))

    gathered, masks = [], []
    for k, piece in enumerate(arrived):
        outer = list(range(1, bits))
        if k % 2 == 0:
            outer = outer[::-1]
        mask = [0]
        for bit in outer + [0]:
            step = 1 << bit
            piece = jnp.concatenate([piece, lax.ppermute(piece, "morton", pairs_xor(segs, step))], axis=0)
            mask = mask + [v ^ step for v in mask]
        gathered.append(piece)
        masks.append(mask)

    smem = pl.BlockSpec(memory_space=pltpu.SMEM)
    vmem = pl.BlockSpec(memory_space=pltpu.VMEM)
    def call(kernel, out, args, scratch=(), flops=0, limit=24 << 20):
        return pl.pallas_call(
            kernel,
            out_shape=out,
            in_specs=[smem] + [vmem] * (len(args) - 1),
            out_specs=vmem,
            scratch_shapes=list(scratch),
            compiler_params=pltpu.CompilerParams(vmem_limit_bytes=limit),
            cost_estimate=pl.CostEstimate(flops=flops, bytes_accessed=1 << 20, transcendentals=0),
        )(*args)

    picked = call(
        functools.partial(gather_kernel, boxes, per, lanes),
        jax.ShapeDtypeStruct((lanes * per, boxes, width), jnp.bfloat16),
        (vec, counts, sources[0].T, relpos[0].T, column, twin, other),
        flops=2 * lanes * per * boxes * boxes * 9 * width,
    )
    buffer = lambda n: [pltpu.VMEM((n, rows, width), jnp.bfloat16)]
    cut = lanes - 2
    before = call(
        functools.partial(early_kernel, masks[:cut], tuple(range(1, cut + 1)), per, width, rows, chunk),
        jax.ShapeDtypeStruct((boxes, width), jnp.float32),
        (vec, picked, operators, *gathered[:cut]),
        buffer(cut),
        flops=2 * boxes * rows * width * (cut + 1),
    )
    density = call(
        functools.partial(late_kernel, masks[cut:], tuple(range(cut + 1, lanes)), per, width, rows, chunk),
        jax.ShapeDtypeStruct((width, boxes), jnp.float32),
        (vec, picked, before, c2e, *gathered[cut:]),
        buffer(lanes - 1 - cut),
        flops=2 * boxes * rows * width,
    )
    return density.T.reshape(1, boxes, width)


def solution(mesh):
    return jax.shard_map(
        per_device,
        mesh=mesh,
        in_specs=(
            P("morton", "lane", None),
            P("morton", "lane"),
            P("morton", "lane", None),
            P("morton", "lane", None),
            P("lane", None, None),
            P(),
        ),
        out_specs=P("morton", "lane", None),
        check_vma=False,
    )
```

```python
import functools

import jax
import jax.numpy as jnp
from jax import lax
from jax.experimental import pallas as pl
from jax.experimental.pallas import tpu as pltpu
from jax.sharding import PartitionSpec as P


def pairs_xor(count, mask):
    return [(i, i ^ mask) for i in range(count)]


def pairs_odd(count):
    out = []
    for i in range(1, count - 1, 2):
        out += [(i, i + 1), (i + 1, i)]
    return out


def part_rows(rows, parts):
    return 8 * -(-rows // (8 * parts))


def part_start(rows, size, index):
    return jnp.minimum(index * size, rows - size)


def gather_kernel(boxes, per, lanes, ids, counts, sources, relpos, column, twin, other, own_hbm, c2e_hbm, out, before, c2e_out, own, sems):
    own_copy = pltpu.make_async_copy(own_hbm, own, sems.at[0])
    c2e_copy = pltpu.make_async_copy(c2e_hbm, c2e_out, sems.at[1])
    own_copy.start()
    c2e_copy.start()
    lane_id, seg_id = ids[0], ids[1]
    code = sources[:, 0, :]
    rel = relpos[:, 0, :]
    width = out.shape[2]
    slot = lax.broadcasted_iota(jnp.int32, rel.shape, 0)
    live = slot < counts[...]
    nb = jnp.zeros_like(code)
    for k in range(1, 9):
        nb = nb + (code >= k * boxes).astype(jnp.int32)
    a = (nb >= 3).astype(jnp.int32) + (nb >= 6).astype(jnp.int32)
    b = nb - 3 * a
    offset = code - nb * boxes

    def place(v, odd):
        return jnp.where(v == 1, 0, jnp.where(v == 2 - 2 * odd, 1, 2))

    mapped = (place(a, seg_id % 2) * 3 + place(b, lane_id % 2)) * boxes + offset + 1
    mapped = jnp.where(live, mapped, 0)
    rows = []
    for g in range(lanes):
        for i in range(per):
            wanted = (lane_id ^ g) * per + i
            rows.append(jnp.sum(jnp.where(rel == wanted, mapped, 0), axis=0, keepdims=True) - 1)
    fill = jnp.full((boxes - len(rows), boxes), -1, jnp.int32)
    index = jnp.concatenate(rows + [fill], axis=0).T
    parts = []
    for ref in (column, twin, other):
        for j in range(3):
            parts.append(ref[pl.ds(j * width, width), :])
    table = jnp.concatenate(parts, axis=1)
    spot = lax.broadcasted_iota(jnp.int32, (boxes, 9 * boxes), 1)
    for g in range(lanes):
        picks = []
        for i in range(per):
            at = g * per + i
            picks.append((index[:, at : at + 1] == spot).astype(jnp.float32).astype(jnp.bfloat16))
        picks = jnp.concatenate(picks, axis=0)
        found = lax.dot_general(picks, table, (((1,), (1,)), ((), ())), preferred_element_type=jnp.float32)
        out[g * per : (g + 1) * per] = found.astype(jnp.bfloat16).reshape(per, boxes, width)
    own_copy.wait()
    total = None
    for i in range(per):
        term = jnp.dot(out[i], own[i], preferred_element_type=jnp.float32)
        total = term if total is None else total + term
    before[...] = total
    c2e_copy.wait()


def accumulate(total, picked, group, buffer, per, width):
    for i in range(per):
        term = jnp.dot(picked[group * per + i], buffer[pl.ds(i * width, width), :], preferred_element_type=jnp.float32)
        total = total + term
    return total


def place_part(buffer, rows, size, index, part):
    buffer[pl.ds(pl.multiple_of(part_start(rows, size, index), 8), size), :] = part


def near_kernel(per, width, ids, picked, before, mine, twin, out, buffer):
    rows, size = per * width, mine.shape[0]
    core = ids[1] % 2
    place_part(buffer, rows, size, core, mine[...])
    place_part(buffer, rows, size, 1 - core, twin[...])
    out[...] = accumulate(before[...], picked, 1, buffer, per, width)


def far_kernel(per, width, count, ids, picked, before, c2e, *refs):
    pieces, twins, out, buffer = refs[:count], refs[count : 2 * count], refs[-2], refs[-1]
    rows = per * width
    groups, size = pieces[0].shape[:2]
    total = before[...]
    for k in range(groups):
        view = buffer.at[k]
        for j in range(count):
            place_part(view, rows, size, ids[1] ^ (2 * j), pieces[j][k])
            place_part(view, rows, size, ids[1] ^ (2 * j + 1), twins[j][k])
        total = accumulate(total, picked, k + 2, view, per, width)
    check = total.astype(jnp.bfloat16)
    out[...] = jnp.dot(check, c2e[...], preferred_element_type=jnp.float32).T


def per_device(multipoles, counts, sources, relpos, operators, c2e):
    segs, lanes = lax.axis_size("morton"), lax.axis_size("lane")
    seg_id, lane_id = lax.axis_index("morton"), lax.axis_index("lane")
    boxes, width = multipoles.shape[1:]
    per = operators.shape[0]
    rows = per * width

    block = multipoles[0].T
    flat = operators.reshape(rows, width)
    half, eighth = part_rows(rows, 2), part_rows(rows, segs)
    near = lax.ppermute(block, "lane", pairs_xor(lanes, 1))
    far = lax.ppermute(block, "lane", pairs_odd(lanes))
    small = lax.dynamic_slice_in_dim(flat, part_start(rows, eighth, seg_id), eighth, 0)[None]
    big = lax.dynamic_slice_in_dim(flat, part_start(rows, half, seg_id % 2), half, 0)
    landed = [lax.ppermute(small, "lane", pairs_xor(lanes, k)) for k in range(2, lanes)]
    mine = lax.ppermute(big, "lane", pairs_xor(lanes, 1))

    column = jnp.concatenate([block, near, far], axis=0)
    twin = lax.ppermute(column, "morton", pairs_xor(segs, 1))
    other = lax.ppermute(column, "morton", pairs_odd(segs))

    landed = jnp.concatenate(landed, axis=0)
    pieces = [landed] + [lax.ppermute(landed, "morton", pairs_xor(segs, 2 * j)) for j in range(1, segs // 2)]
    mine_twin = lax.ppermute(mine, "morton", pairs_xor(segs, 1))
    twins = [lax.ppermute(piece, "morton", pairs_xor(segs, 1)) for piece in pieces]

    smem = pl.BlockSpec(memory_space=pltpu.SMEM)
    vmem = pl.BlockSpec(memory_space=pltpu.VMEM)
    anywhere = pl.BlockSpec(memory_space=pl.ANY)

    def call(kernel, out, args, specs=None, scratch=(), flops=0, limit=24 << 20):
        return pl.pallas_call(
            kernel,
            out_shape=out,
            in_specs=[smem] + (specs or [vmem] * (len(args) - 1)),
            out_specs=jax.tree.map(lambda _: vmem, out),
            scratch_shapes=list(scratch),
            compiler_params=pltpu.CompilerParams(vmem_limit_bytes=limit),
            cost_estimate=pl.CostEstimate(flops=flops, bytes_accessed=1 << 20, transcendentals=0),
        )(*args)

    vec = jnp.stack([lane_id, seg_id]).astype(jnp.int32)
    sums = jax.ShapeDtypeStruct((boxes, width), jnp.float32)
    picked, before, c2e_near = call(
        functools.partial(gather_kernel, boxes, per, lanes),
        (
            jax.ShapeDtypeStruct((lanes * per, boxes, width), jnp.bfloat16),
            sums,
            jax.ShapeDtypeStruct(c2e.shape, c2e.dtype),
        ),
        (vec, counts, jnp.transpose(sources, (2, 0, 1)), jnp.transpose(relpos, (2, 0, 1)), column, twin, other, operators, c2e),
        specs=[vmem] * 6 + [anywhere] * 2,
        scratch=[pltpu.VMEM(operators.shape, operators.dtype), pltpu.SemaphoreType.DMA((2,))],
        flops=2 * lanes * per * boxes * boxes * 9 * width,
    )
    before = call(
        functools.partial(near_kernel, per, width),
        sums,
        (vec, picked, before, mine, mine_twin),
        scratch=[pltpu.VMEM((rows, width), jnp.bfloat16)],
        flops=2 * boxes * rows * width,
    )
    density = call(
        functools.partial(far_kernel, per, width, len(pieces)),
        jax.ShapeDtypeStruct((width, boxes), jnp.float32),
        (vec, picked, before, c2e_near, *pieces, *twins),
        scratch=[pltpu.VMEM((lanes - 2, rows, width), jnp.bfloat16)],
        flops=2 * boxes * rows * width,
    )
    return density.T.reshape(1, boxes, width)


def solution(mesh):
    return jax.shard_map(
        per_device,
        mesh=mesh,
        in_specs=(
            P("morton", "lane", None),
            P("morton", "lane"),
            P("morton", "lane", None),
            P("morton", "lane", None),
            P("lane", None, None),
            P(),
        ),
        out_specs=P("morton", "lane", None),
        check_vma=False,
    )
```

```python
import functools

import jax
import jax.numpy as jnp
from jax import lax
from jax.experimental import pallas as pl
from jax.experimental.pallas import tpu as pltpu
from jax.sharding import PartitionSpec as P


def pairs_xor(count, mask):
    return [(i, i ^ mask) for i in range(count)]


def pairs_odd(count):
    out = []
    for i in range(1, count - 1, 2):
        out += [(i, i + 1), (i + 1, i)]
    return out


def part_rows(rows, parts):
    return 8 * -(-rows // (8 * parts))


def part_start(rows, size, index):
    return jnp.minimum(index * size, rows - size)


def prep_kernel(rows, ids, flat, block, small, block_out, sems):
    size = small.shape[1]
    start = pl.multiple_of(part_start(rows, size, ids[1]), 8)
    copies = [
        pltpu.make_async_copy(flat.at[pl.ds(start, size), :], small.at[0], sems.at[0]),
        pltpu.make_async_copy(block, block_out, sems.at[1]),
    ]
    for copy in copies:
        copy.start()
    for copy in copies:
        copy.wait()


def side_tables(refs, width):
    parts = []
    for ref in refs:
        for j in range(3):
            parts.append(ref[pl.ds(j * width, width), :])
    return jnp.concatenate(parts, axis=1)


def pick_rows(index, table, first, group, per, boxes):
    spot = lax.broadcasted_iota(jnp.int32, (boxes, table.shape[1]), 1) + first
    picks = []
    for i in range(per):
        at = group * per + i
        picks.append((index[:, at : at + 1] == spot).astype(jnp.float32).astype(jnp.bfloat16))
    picks = jnp.concatenate(picks, axis=0)
    found = lax.dot_general(picks, table, (((1,), (1,)), ((), ())), preferred_element_type=jnp.float32)
    return found.astype(jnp.bfloat16).reshape(per, boxes, table.shape[0])


def first_kernel(boxes, per, lanes, ids, counts, sources, relpos, column, c2e, out, index_out, c2e_out):
    lane_id, seg_id = ids[0], ids[1]
    code = sources[:, 0, :]
    rel = relpos[:, 0, :]
    slot = lax.broadcasted_iota(jnp.int32, rel.shape, 0)
    live = slot < counts[...]
    nb = jnp.zeros_like(code)
    for k in range(1, 9):
        nb = nb + (code >= k * boxes).astype(jnp.int32)
    a = (nb >= 3).astype(jnp.int32) + (nb >= 6).astype(jnp.int32)
    b = nb - 3 * a
    offset = code - nb * boxes

    def place(v, odd):
        return jnp.where(v == 1, 0, jnp.where(v == 2 - 2 * odd, 1, 2))

    mapped = (place(b, lane_id % 2) * 3 + place(a, seg_id % 2)) * boxes + offset + 1
    mapped = jnp.where(live, mapped, 0)
    rows = []
    for g in range(lanes):
        for i in range(per):
            wanted = (lane_id ^ g) * per + i
            rows.append(jnp.sum(jnp.where(rel == wanted, mapped, 0), axis=0, keepdims=True) - 1)
    fill = jnp.full((boxes - len(rows), boxes), -1, jnp.int32)
    index = jnp.concatenate(rows + [fill], axis=0).T
    index_out[...] = index
    table = side_tables((column,), out.shape[2])
    for g in range(lanes):
        out[g * per : (g + 1) * per] = pick_rows(index, table, 0, g, per, boxes)
    c2e_out[...] = c2e[...]


def second_kernel(boxes, per, lanes, index, part, near, far, own, out, before):
    table = side_tables((near, far), out.shape[2])
    values = index[...]
    total = None
    for g in range(lanes):
        at = slice(g * per, (g + 1) * per)
        found = part[at] + pick_rows(values, table, 3 * boxes, g, per, boxes)
        out[at] = found
        if g == 0:
            for i in range(per):
                term = jnp.dot(found[i], own[i], preferred_element_type=jnp.float32)
                total = term if total is None else total + term
    before[...] = total


def accumulate(total, picked, group, buffer, per, width):
    for i in range(per):
        term = jnp.dot(picked[group * per + i], buffer[pl.ds(i * width, width), :], preferred_element_type=jnp.float32)
        total = total + term
    return total


def place_part(buffer, rows, size, index, part):
    buffer[pl.ds(pl.multiple_of(part_start(rows, size, index), 8), size), :] = part


def far_kernel(per, width, count, ids, picked, before, c2e, *refs):
    pieces, twins, out, buffer = refs[:count], refs[count : 2 * count], refs[-2], refs[-1]
    rows = per * width
    groups, size = pieces[0].shape[:2]
    total = before[...]
    for k in range(groups):
        view = buffer.at[k]
        for j in range(count):
            place_part(view, rows, size, ids[1] ^ (2 * j), pieces[j][k])
            place_part(view, rows, size, ids[1] ^ (2 * j + 1), twins[j][k])
        total = accumulate(total, picked, k + 1, view, per, width)
    check = total.astype(jnp.bfloat16)
    out[...] = jnp.dot(check, c2e[...], preferred_element_type=jnp.float32).T


def per_device(multipoles, counts, sources, relpos, operators, c2e):
    segs, lanes = lax.axis_size("morton"), lax.axis_size("lane")
    seg_id, lane_id = lax.axis_index("morton"), lax.axis_index("lane")
    boxes, width = multipoles.shape[1:]
    per = operators.shape[0]
    rows = per * width

    block = multipoles[0].T
    flat = operators.reshape(rows, width)
    eighth = part_rows(rows, segs)
    smem = pl.BlockSpec(memory_space=pltpu.SMEM)
    vmem = pl.BlockSpec(memory_space=pltpu.VMEM)
    hbm = pl.BlockSpec(memory_space=pltpu.HBM)

    def call(kernel, out, args, specs=None, scratch=(), flops=0, limit=24 << 20):
        return pl.pallas_call(
            kernel,
            out_shape=out,
            in_specs=specs or [smem] + [vmem] * (len(args) - 1),
            out_specs=jax.tree.map(lambda _: vmem, out),
            scratch_shapes=list(scratch),
            compiler_params=pltpu.CompilerParams(vmem_limit_bytes=limit),
            cost_estimate=pl.CostEstimate(flops=flops, bytes_accessed=1 << 20, transcendentals=0),
        )(*args)

    vec = jnp.stack([lane_id, seg_id]).astype(jnp.int32)
    small, block_near = call(
        functools.partial(prep_kernel, rows),
        (
            jax.ShapeDtypeStruct((1, eighth, width), operators.dtype),
            jax.ShapeDtypeStruct(block.shape, block.dtype),
        ),
        (vec, pltpu.with_memory_space_constraint(flat, pltpu.HBM), pltpu.with_memory_space_constraint(block, pltpu.HBM)),
        specs=[smem, hbm, hbm],
        scratch=[pltpu.SemaphoreType.DMA((2,))],
    )
    twin = lax.ppermute(block, "morton", pairs_xor(segs, 1))
    other = lax.ppermute(block, "morton", pairs_odd(segs))
    column = jnp.concatenate([block_near, twin, other], axis=0)
    near = lax.ppermute(column, "lane", pairs_xor(lanes, 1))
    far = lax.ppermute(column, "lane", pairs_odd(lanes))
    landed = [lax.ppermute(small, "lane", pairs_xor(lanes, k)) for k in range(1, lanes)]

    landed = jnp.concatenate(landed, axis=0)
    pieces = [landed]
    while len(pieces) < segs // 2:
        step = len(pieces)
        pieces += [lax.ppermute(piece, "morton", pairs_xor(segs, 2 * step)) for piece in pieces]
    twins = [lax.ppermute(piece, "morton", pairs_xor(segs, 1)) for piece in pieces]

    sums = jax.ShapeDtypeStruct((boxes, width), jnp.float32)
    table = jax.ShapeDtypeStruct((lanes * per, boxes, width), jnp.bfloat16)
    part, index, c2e_near = call(
        functools.partial(first_kernel, boxes, per, lanes),
        (table, jax.ShapeDtypeStruct((boxes, boxes), jnp.int32), jax.ShapeDtypeStruct(c2e.shape, c2e.dtype)),
        (vec, counts, jnp.transpose(sources, (2, 0, 1)), jnp.transpose(relpos, (2, 0, 1)), column, c2e),
        flops=2 * lanes * per * boxes * boxes * 3 * width,
    )
    picked, before = call(
        functools.partial(second_kernel, boxes, per, lanes),
        (table, sums),
        (index, part, near, far, operators),
        specs=[vmem] * 5,
        flops=2 * lanes * per * boxes * boxes * 6 * width,
    )
    density = call(
        functools.partial(far_kernel, per, width, len(pieces)),
        jax.ShapeDtypeStruct((width, boxes), jnp.float32),
        (vec, picked, before, c2e_near, *pieces, *twins),
        scratch=[pltpu.VMEM((lanes - 1, rows, width), jnp.bfloat16)],
        flops=2 * lanes * boxes * rows * width,
    )
    return density.T.reshape(1, boxes, width)


def solution(mesh):
    return jax.shard_map(
        per_device,
        mesh=mesh,
        in_specs=(
            P("morton", "lane", None),
            P("morton", "lane"),
            P("morton", "lane", None),
            P("morton", "lane", None),
            P("lane", None, None),
            P(),
        ),
        out_specs=P("morton", "lane", None),
        check_vma=False,
    )
```

```python
import functools

import jax
import jax.numpy as jnp
from jax import lax
from jax.experimental import pallas as pl
from jax.experimental.pallas import tpu as pltpu
from jax.sharding import PartitionSpec as P


def pairs_xor(count, mask):
    return [(i, i ^ mask) for i in range(count)]


def pairs_odd(count):
    out = []
    for i in range(1, count - 1, 2):
        out += [(i, i + 1), (i + 1, i)]
    return out


def part_rows(rows, parts):
    return 8 * -(-rows // (8 * parts))


def part_start(rows, size, index):
    return jnp.minimum(index * size, rows - size)


def prep_kernel(rows, ids, flat, block, small, mid, block_out, sems):
    copies = []
    for at, (out, parts) in enumerate(((small, None), (mid, 2))):
        size = out.shape[1]
        index = ids[1] if parts is None else ids[1] % parts
        start = pl.multiple_of(part_start(rows, size, index), 8)
        copies.append(pltpu.make_async_copy(flat.at[pl.ds(start, size), :], out.at[0], sems.at[at]))
    copies.append(pltpu.make_async_copy(block, block_out, sems.at[2]))
    for copy in copies:
        copy.start()
    for copy in copies:
        copy.wait()


def side_tables(refs, width):
    parts = []
    for ref in refs:
        for j in range(3):
            parts.append(ref[pl.ds(j * width, width), :])
    return jnp.concatenate(parts, axis=1)


def pick_rows(index, table, first, group, per, boxes):
    spot = lax.broadcasted_iota(jnp.int32, (boxes, table.shape[1]), 1) + first
    picks = []
    for i in range(per):
        at = group * per + i
        picks.append((index[:, at : at + 1] == spot).astype(jnp.float32).astype(jnp.bfloat16))
    picks = jnp.concatenate(picks, axis=0)
    found = lax.dot_general(picks, table, (((1,), (1,)), ((), ())), preferred_element_type=jnp.float32)
    return found.astype(jnp.bfloat16).reshape(per, boxes, table.shape[0])


def first_kernel(boxes, per, lanes, ids, counts, sources, relpos, column, c2e, out, index_out, c2e_out):
    lane_id, seg_id = ids[0], ids[1]
    code = sources[:, 0, :]
    rel = relpos[:, 0, :]
    slot = lax.broadcasted_iota(jnp.int32, rel.shape, 0)
    live = slot < counts[...]
    nb = jnp.zeros_like(code)
    for k in range(1, 9):
        nb = nb + (code >= k * boxes).astype(jnp.int32)
    a = (nb >= 3).astype(jnp.int32) + (nb >= 6).astype(jnp.int32)
    b = nb - 3 * a
    offset = code - nb * boxes

    def place(v, odd):
        return jnp.where(v == 1, 0, jnp.where(v == 2 - 2 * odd, 1, 2))

    mapped = (place(b, lane_id % 2) * 3 + place(a, seg_id % 2)) * boxes + offset + 1
    mapped = jnp.where(live, mapped, 0)
    rows = []
    for g in range(lanes):
        for i in range(per):
            wanted = (lane_id ^ g) * per + i
            rows.append(jnp.sum(jnp.where(rel == wanted, mapped, 0), axis=0, keepdims=True) - 1)
    fill = jnp.full((boxes - len(rows), boxes), -1, jnp.int32)
    index = jnp.concatenate(rows + [fill], axis=0).T
    index_out[...] = index
    table = side_tables((column,), out.shape[2])
    for g in range(lanes):
        out[g * per : (g + 1) * per] = pick_rows(index, table, 0, g, per, boxes)
    c2e_out[...] = c2e[...]


def second_kernel(boxes, per, lanes, index, part, near, far, own, out, before):
    table = side_tables((near, far), out.shape[2])
    values = index[...]
    total = None
    for g in range(lanes):
        at = slice(g * per, (g + 1) * per)
        found = part[at] + pick_rows(values, table, 3 * boxes, g, per, boxes)
        out[at] = found
        if g == 0:
            for i in range(per):
                term = jnp.dot(found[i], own[i], preferred_element_type=jnp.float32)
                total = term if total is None else total + term
    before[...] = total


def accumulate(total, picked, group, buffer, per, width):
    for i in range(per):
        term = jnp.dot(picked[group * per + i], buffer[pl.ds(i * width, width), :], preferred_element_type=jnp.float32)
        total = total + term
    return total


def place_part(buffer, rows, size, index, part):
    buffer[pl.ds(pl.multiple_of(part_start(rows, size, index), 8), size), :] = part


def far_kernel(per, width, count, ids, picked, before, c2e, close, close_twin, *refs):
    pieces, twins, out, buffer = refs[:count], refs[count : 2 * count], refs[-2], refs[-1]
    rows = per * width
    groups, size = pieces[0].shape[:2]
    view = buffer.at[0]
    for other, part in enumerate((close, close_twin)):
        place_part(view, rows, part.shape[1], (ids[1] ^ other) % 2, part[0])
    total = accumulate(before[...], picked, 1, view, per, width)
    for k in range(groups):
        view = buffer.at[k + 1]
        for j in range(count):
            place_part(view, rows, size, ids[1] ^ (2 * j), pieces[j][k])
            place_part(view, rows, size, ids[1] ^ (2 * j + 1), twins[j][k])
        total = accumulate(total, picked, k + 2, view, per, width)
    check = total.astype(jnp.bfloat16)
    out[...] = jnp.dot(check, c2e[...], preferred_element_type=jnp.float32).T


def per_device(multipoles, counts, sources, relpos, operators, c2e):
    segs, lanes = lax.axis_size("morton"), lax.axis_size("lane")
    seg_id, lane_id = lax.axis_index("morton"), lax.axis_index("lane")
    boxes, width = multipoles.shape[1:]
    per = operators.shape[0]
    rows = per * width

    block = multipoles[0].T
    flat = operators.reshape(rows, width)
    eighth, quarter = part_rows(rows, segs), part_rows(rows, 2)
    smem = pl.BlockSpec(memory_space=pltpu.SMEM)
    vmem = pl.BlockSpec(memory_space=pltpu.VMEM)
    hbm = pl.BlockSpec(memory_space=pltpu.HBM)

    def call(kernel, out, args, specs=None, scratch=(), flops=0, limit=24 << 20):
        return pl.pallas_call(
            kernel,
            out_shape=out,
            in_specs=specs or [smem] + [vmem] * (len(args) - 1),
            out_specs=jax.tree.map(lambda _: vmem, out),
            scratch_shapes=list(scratch),
            compiler_params=pltpu.CompilerParams(vmem_limit_bytes=limit),
            cost_estimate=pl.CostEstimate(flops=flops, bytes_accessed=1 << 20, transcendentals=0),
        )(*args)

    vec = jnp.stack([lane_id, seg_id]).astype(jnp.int32)
    small, mid, block_near = call(
        functools.partial(prep_kernel, rows),
        (
            jax.ShapeDtypeStruct((1, eighth, width), operators.dtype),
            jax.ShapeDtypeStruct((1, quarter, width), operators.dtype),
            jax.ShapeDtypeStruct(block.shape, block.dtype),
        ),
        (vec, pltpu.with_memory_space_constraint(flat, pltpu.HBM), pltpu.with_memory_space_constraint(block, pltpu.HBM)),
        specs=[smem, hbm, hbm],
        scratch=[pltpu.SemaphoreType.DMA((3,))],
    )
    twin = lax.ppermute(block, "morton", pairs_xor(segs, 1))
    other = lax.ppermute(block, "morton", pairs_odd(segs))
    column = jnp.concatenate([block_near, twin, other], axis=0)
    near = lax.ppermute(column, "lane", pairs_xor(lanes, 1))
    far = lax.ppermute(column, "lane", pairs_odd(lanes))
    landed = [lax.ppermute(small, "lane", pairs_xor(lanes, k)) for k in range(2, lanes)]
    close = lax.ppermute(mid, "lane", pairs_xor(lanes, 1))

    landed = jnp.concatenate(landed, axis=0)
    pieces = [landed]
    while len(pieces) < segs // 2:
        step = len(pieces)
        pieces += [lax.ppermute(piece, "morton", pairs_xor(segs, 2 * step)) for piece in pieces]
    close_twin = lax.ppermute(close, "morton", pairs_xor(segs, 1))
    twins = [lax.ppermute(piece, "morton", pairs_xor(segs, 1)) for piece in pieces]

    sums = jax.ShapeDtypeStruct((boxes, width), jnp.float32)
    table = jax.ShapeDtypeStruct((lanes * per, boxes, width), jnp.bfloat16)
    part, index, c2e_near = call(
        functools.partial(first_kernel, boxes, per, lanes),
        (table, jax.ShapeDtypeStruct((boxes, boxes), jnp.int32), jax.ShapeDtypeStruct(c2e.shape, c2e.dtype)),
        (vec, counts, jnp.transpose(sources, (2, 0, 1)), jnp.transpose(relpos, (2, 0, 1)), column, c2e),
        flops=2 * lanes * per * boxes * boxes * 3 * width,
    )
    picked, before = call(
        functools.partial(second_kernel, boxes, per, lanes),
        (table, sums),
        (index, part, near, far, operators),
        specs=[vmem] * 5,
        flops=2 * lanes * per * boxes * boxes * 6 * width,
    )
    density = call(
        functools.partial(far_kernel, per, width, len(pieces)),
        jax.ShapeDtypeStruct((width, boxes), jnp.float32),
        (vec, picked, before, c2e_near, close, close_twin, *pieces, *twins),
        scratch=[pltpu.VMEM((lanes - 1, rows, width), jnp.bfloat16)],
        flops=2 * lanes * boxes * rows * width,
    )
    return density.T.reshape(1, boxes, width)


def solution(mesh):
    return jax.shard_map(
        per_device,
        mesh=mesh,
        in_specs=(
            P("morton", "lane", None),
            P("morton", "lane"),
            P("morton", "lane", None),
            P("morton", "lane", None),
            P("lane", None, None),
            P(),
        ),
        out_specs=P("morton", "lane", None),
        check_vma=False,
    )
```

```python
import functools

import jax
import jax.numpy as jnp
from jax import lax
from jax.experimental import pallas as pl
from jax.experimental.pallas import tpu as pltpu
from jax.sharding import PartitionSpec as P


def pairs_xor(count, mask):
    return [(i, i ^ mask) for i in range(count)]


def pairs_odd(count):
    out = []
    for i in range(1, count - 1, 2):
        out += [(i, i + 1), (i + 1, i)]
    return out


def part_rows(rows, parts):
    return 16 * -(-rows // (16 * parts))


def copy_part(flat, out, size, index, sem, act):
    rows = flat.shape[0]
    whole, rest = divmod(rows, size)

    def move(count):
        start = pl.multiple_of(index * size, 16)
        copy = pltpu.make_async_copy(flat.at[pl.ds(start, count), :], out.at[pl.ds(0, count), :], sem)
        copy.start() if act == "start" else copy.wait()

    pl.when(index < whole)(lambda: move(size))
    if rest:
        pl.when(index == whole)(lambda: move(rest))


def prep_kernel(flat, block, small, mid, block_out, sems):
    seg_id = lax.axis_index("morton")

    def parts(act):
        for at, (out, index) in enumerate(((small, seg_id), (mid, seg_id % 2))):
            copy_part(flat, out.at[0], out.shape[1], index, sems.at[at], act)

    whole = pltpu.make_async_copy(block, block_out, sems.at[2])
    parts("start")
    whole.start()
    parts("wait")
    whole.wait()


def side_tables(refs, width):
    parts = []
    for ref in refs:
        for j in range(3):
            parts.append(ref[pl.ds(j * width, width), :])
    return jnp.concatenate(parts, axis=1)


def pick_rows(index, table, first, at, count, boxes):
    spot = lax.broadcasted_iota(jnp.int32, (table.shape[1], boxes), 0) + first
    picks = [(index[at + i : at + i + 1, :] == spot).astype(jnp.float32).astype(jnp.bfloat16) for i in range(count)]
    picks = jnp.concatenate(picks, axis=1) if count > 1 else picks[0]
    return jnp.dot(table, picks, preferred_element_type=jnp.float32).astype(jnp.bfloat16)


def first_kernel(boxes, per, lanes, counts, sources, relpos, column, c2e, out, index_out, c2e_out):
    lane_id, seg_id = lax.axis_index("lane"), lax.axis_index("morton")
    code = sources[:, 0, :]
    rel = relpos[:, 0, :]
    slot = lax.broadcasted_iota(jnp.int32, rel.shape, 0)
    live = slot < counts[...]
    nb = jnp.zeros_like(code)
    for k in range(1, 9):
        nb = nb + (code >= k * boxes).astype(jnp.int32)
    a = (nb >= 3).astype(jnp.int32) + (nb >= 6).astype(jnp.int32)
    b = nb - 3 * a
    offset = code - nb * boxes

    def place(v, odd):
        return jnp.where(v == 1, 0, jnp.where(v == 2 - 2 * odd, 1, 2))

    mapped = (place(b, lane_id % 2) * 3 + place(a, seg_id % 2)) * boxes + offset + 1
    mapped = jnp.where(live, mapped, 0)
    rows = []
    for g in range(lanes):
        for i in range(per):
            wanted = (lane_id ^ g) * per + i
            rows.append(jnp.sum(jnp.where(rel == wanted, mapped, 0), axis=0, keepdims=True) - 1)
    index = jnp.concatenate(rows, axis=0)
    index_out[...] = index
    table = side_tables((column,), out.shape[1])
    for at in range(0, len(rows), 2):
        count = min(2, len(rows) - at)
        found = pick_rows(index, table, 0, at, count, boxes)
        for i in range(count):
            out[at + i] = found[:, i * boxes : (i + 1) * boxes]
    c2e_out[...] = c2e[...]


def second_kernel(boxes, index, part, near, far, out):
    table = side_tables((near, far), out.shape[2])
    values = index[...]
    total = values.shape[0]
    for at in range(0, total, 2):
        count = min(2, total - at)
        found = pick_rows(values, table, 3 * boxes, at, count, boxes)
        for i in range(count):
            out[at + i] = (part[at + i] + found[:, i * boxes : (i + 1) * boxes]).T


def accumulate(total, picked, group, buffer, per, width):
    for i in range(per):
        term = jnp.dot(picked[group * per + i], buffer[pl.ds(i * width, width), :], preferred_element_type=jnp.float32)
        total = total + term
    return total


def place_part(buffer, index, part):
    size = part.shape[0]
    buffer[pl.ds(pl.multiple_of(index * size, 16), size), :] = part


def place_pieces(buffer, seg_id, first, pieces, twins):
    for k in range(pieces[0].shape[0]):
        for j, (piece, twin) in enumerate(zip(pieces, twins)):
            place_part(buffer.at[k], seg_id ^ (2 * (first + j)), piece[k])
            place_part(buffer.at[k], seg_id ^ (2 * (first + j) + 1), twin[k])


def mid_kernel(per, width, count, picked, own, close, close_twin, *refs):
    pieces, twins = refs[:count], refs[count : 2 * count]
    before, buffer, near = refs[2 * count :]
    seg_id = lax.axis_index("morton")
    core = seg_id % 2
    place_part(near, core, close[0])
    place_part(near, 1 - core, close_twin[0])
    total = None
    for i in range(per):
        term = jnp.dot(picked[i], own[i], preferred_element_type=jnp.float32)
        total = term if total is None else total + term
    before[...] = accumulate(total, picked, 1, near, per, width)
    place_pieces(buffer, seg_id, 0, pieces, twins)


def far_kernel(per, width, first, picked, before, c2e, piece, twin, filled, out, buffer):
    place_pieces(buffer, lax.axis_index("morton"), first, [piece], [twin])
    total = before[...]
    for k in range(buffer.shape[0]):
        total = accumulate(total, picked, k + 2, buffer.at[k], per, width)
    check = total.astype(jnp.bfloat16)
    out[...] = jnp.dot(check, c2e[...], preferred_element_type=jnp.float32).T


def per_device(multipoles, counts, sources, relpos, operators, c2e):
    segs, lanes = lax.axis_size("morton"), lax.axis_size("lane")
    boxes, width = multipoles.shape[1:]
    per = operators.shape[0]
    rows = per * width

    block = multipoles[0].T
    flat = operators.reshape(rows, width)
    eighth, quarter = part_rows(rows, segs), part_rows(rows, 2)
    vmem = pl.BlockSpec(memory_space=pltpu.VMEM)
    hbm = pl.BlockSpec(memory_space=pltpu.HBM)

    def call(kernel, out, args, specs=None, scratch=(), flops=0, limit=24 << 20, alias=None):
        return pl.pallas_call(
            kernel,
            out_shape=out,
            in_specs=specs or [vmem] * len(args),
            out_specs=jax.tree.map(lambda _: vmem, out),
            scratch_shapes=list(scratch),
            input_output_aliases=alias or {},
            compiler_params=pltpu.CompilerParams(vmem_limit_bytes=limit),
            cost_estimate=pl.CostEstimate(flops=flops, bytes_accessed=1 << 20, transcendentals=0),
        )(*args)

    small, mid, block_near = call(
        prep_kernel,
        (
            jax.ShapeDtypeStruct((1, eighth, width), operators.dtype),
            jax.ShapeDtypeStruct((1, quarter, width), operators.dtype),
            jax.ShapeDtypeStruct(block.shape, block.dtype),
        ),
        (pltpu.with_memory_space_constraint(flat, pltpu.HBM), pltpu.with_memory_space_constraint(block, pltpu.HBM)),
        specs=[hbm, hbm],
        scratch=[pltpu.SemaphoreType.DMA((3,))],
    )
    twin = lax.ppermute(block, "morton", pairs_xor(segs, 1))
    other = lax.ppermute(block, "morton", pairs_odd(segs))
    column = jnp.concatenate([block_near, twin, other], axis=0)
    near = lax.ppermute(column, "lane", pairs_xor(lanes, 1))
    far = lax.ppermute(column, "lane", pairs_odd(lanes))
    landed = [lax.ppermute(small, "lane", pairs_xor(lanes, k)) for k in range(2, lanes)]
    close = lax.ppermute(mid, "lane", pairs_xor(lanes, 1))

    landed = jnp.concatenate(landed, axis=0)
    pieces = [landed]
    while len(pieces) < segs // 2:
        step = len(pieces)
        pieces += [lax.ppermute(piece, "morton", pairs_xor(segs, 2 * step)) for piece in pieces]
    close_twin = lax.ppermute(close, "morton", pairs_xor(segs, 1))
    twins = [lax.ppermute(piece, "morton", pairs_xor(segs, 1)) for piece in pieces]

    sums = jax.ShapeDtypeStruct((boxes, width), jnp.float32)
    total = lanes * per
    part, index, c2e_near = call(
        functools.partial(first_kernel, boxes, per, lanes),
        (
            jax.ShapeDtypeStruct((total, width, boxes), jnp.bfloat16),
            jax.ShapeDtypeStruct((total, boxes), jnp.int32),
            jax.ShapeDtypeStruct(c2e.shape, c2e.dtype),
        ),
        (counts, jnp.transpose(sources, (2, 0, 1)), jnp.transpose(relpos, (2, 0, 1)), column, c2e),
        flops=2 * total * boxes * boxes * 3 * width,
    )
    picked = call(
        functools.partial(second_kernel, boxes),
        jax.ShapeDtypeStruct((total, boxes, width), jnp.bfloat16),
        (index, part, near, far),
        specs=[vmem] * 4,
        flops=2 * total * boxes * boxes * 6 * width,
    )
    buffer = jax.ShapeDtypeStruct((lanes - 2, eighth * segs, width), jnp.bfloat16)
    early = len(pieces) - 1
    before, buffer_mid = call(
        functools.partial(mid_kernel, per, width, early),
        (sums, buffer),
        (picked, operators, close, close_twin, *pieces[:early], *twins[:early]),
        scratch=[pltpu.VMEM((2 * quarter, width), jnp.bfloat16)],
        flops=4 * boxes * rows * width,
    )
    density, _ = call(
        functools.partial(far_kernel, per, width, early),
        (jax.ShapeDtypeStruct((width, boxes), jnp.float32), buffer),
        (picked, before, c2e_near, pieces[early], twins[early], buffer_mid),
        alias={5: 1},
        flops=2 * lanes * boxes * rows * width,
    )
    return density.T.reshape(1, boxes, width)


def solution(mesh):
    return jax.shard_map(
        per_device,
        mesh=mesh,
        in_specs=(
            P("morton", "lane", None),
            P("morton", "lane"),
            P("morton", "lane", None),
            P("morton", "lane", None),
            P("lane", None, None),
            P(),
        ),
        out_specs=P("morton", "lane", None),
        check_vma=False,
    )
```

```python
import functools

import jax
import jax.numpy as jnp
from jax import lax
from jax.experimental import pallas as pl
from jax.experimental.pallas import tpu as pltpu
from jax.sharding import PartitionSpec as P


def pairs_xor(count, mask):
    return [(i, i ^ mask) for i in range(count)]


def pairs_odd(count):
    out = [(0, count - 1), (count - 1, 0)]
    for i in range(1, count - 1, 2):
        out += [(i, i + 1), (i + 1, i)]
    return out


def pairs_far(segs, lanes):
    ends = (0, lanes - 1)
    out = [(i * lanes + j, (i ^ 1) * lanes + j) for i in range(segs) for j in ends]
    for i, j in pairs_odd(lanes):
        if i not in ends:
            out += [(k * lanes + i, k * lanes + j) for k in range(segs)]
    return out


def part_rows(rows, parts):
    return 16 * -(-rows // (16 * parts))


def copy_part(flat, out, size, index, sem, act):
    rows = flat.shape[0]
    whole, rest = divmod(rows, size)

    def move(count):
        start = pl.multiple_of(index * size, 16)
        copy = pltpu.make_async_copy(flat.at[pl.ds(start, count), :], out.at[pl.ds(0, count), :], sem)
        copy.start() if act == "start" else copy.wait()

    pl.when(index < whole)(lambda: move(size))
    if rest:
        pl.when(index == whole)(lambda: move(rest))


def prep_kernel(flat, block, small, mid, block_out, sems):
    seg_id = lax.axis_index("morton")

    def parts(act):
        for at, (out, index) in enumerate(((small, seg_id), (mid, seg_id % 2))):
            copy_part(flat, out.at[0], out.shape[1], index, sems.at[at], act)

    whole = pltpu.make_async_copy(block, block_out, sems.at[2])
    parts("start")
    whole.start()
    parts("wait")
    whole.wait()


def side_tables(refs, width):
    parts = []
    for ref in refs:
        for j in range(3):
            parts.append(ref[pl.ds(j * width, width), :])
    return jnp.concatenate(parts, axis=1)


def pick_rows(index, table, first, at, count, boxes):
    spot = lax.broadcasted_iota(jnp.int32, (table.shape[1], boxes), 0) + first
    picks = [(index[at + i : at + i + 1, :] == spot).astype(jnp.float32).astype(jnp.bfloat16) for i in range(count)]
    picks = jnp.concatenate(picks, axis=1) if count > 1 else picks[0]
    return jnp.dot(table, picks, preferred_element_type=jnp.float32).astype(jnp.bfloat16)


def first_kernel(boxes, per, lanes, counts, sources, relpos, column, c2e, out, index_out, c2e_out):
    lane_id, seg_id = lax.axis_index("lane"), lax.axis_index("morton")
    code = sources[:, 0, :]
    rel = relpos[:, 0, :]
    slot = lax.broadcasted_iota(jnp.int32, rel.shape, 0)
    live = slot < counts[...]
    nb = jnp.zeros_like(code)
    for k in range(1, 9):
        nb = nb + (code >= k * boxes).astype(jnp.int32)
    a = (nb >= 3).astype(jnp.int32) + (nb >= 6).astype(jnp.int32)
    b = nb - 3 * a
    offset = code - nb * boxes

    def place(v, odd):
        return jnp.where(v == 1, 0, jnp.where(v == 2 - 2 * odd, 1, 2))

    mapped = (place(b, lane_id % 2) * 3 + place(a, seg_id % 2)) * boxes + offset + 1
    mapped = jnp.where(live, mapped, 0)
    rows = []
    for g in range(lanes):
        for i in range(per):
            wanted = (lane_id ^ g) * per + i
            rows.append(jnp.sum(jnp.where(rel == wanted, mapped, 0), axis=0, keepdims=True) - 1)
    index = jnp.concatenate(rows, axis=0)
    index_out[...] = index
    table = side_tables((column,), out.shape[1])
    for at in range(0, len(rows), 2):
        count = min(2, len(rows) - at)
        found = pick_rows(index, table, 0, at, count, boxes)
        for i in range(count):
            out[at + i] = found[:, i * boxes : (i + 1) * boxes]
    c2e_out[...] = c2e[...]


def second_kernel(boxes, index, part, near, far, out):
    table = side_tables((near, far), out.shape[2])
    values = index[...]
    total = values.shape[0]
    for at in range(0, total, 2):
        count = min(2, total - at)
        found = pick_rows(values, table, 3 * boxes, at, count, boxes)
        for i in range(count):
            out[at + i] = (part[at + i] + found[:, i * boxes : (i + 1) * boxes]).T


def accumulate(total, picked, group, buffer, per, width):
    for i in range(per):
        term = jnp.dot(picked[group * per + i], buffer[pl.ds(i * width, width), :], preferred_element_type=jnp.float32)
        total = total + term
    return total


def place_part(buffer, index, part):
    size = part.shape[0]
    buffer[pl.ds(pl.multiple_of(index * size, 16), size), :] = part


def place_pieces(buffer, seg_id, first, pieces, twins):
    for k in range(pieces[0].shape[0]):
        for j, (piece, twin) in enumerate(zip(pieces, twins)):
            place_part(buffer.at[k], seg_id ^ (2 * (first + j)), piece[k])
            place_part(buffer.at[k], seg_id ^ (2 * (first + j) + 1), twin[k])


def mid_kernel(per, width, count, picked, own, close, close_twin, *refs):
    pieces, twins = refs[:count], refs[count : 2 * count]
    before, buffer, near = refs[2 * count :]
    seg_id = lax.axis_index("morton")
    core = seg_id % 2
    place_part(near, core, close[0])
    place_part(near, 1 - core, close_twin[0])
    total = None
    for i in range(per):
        term = jnp.dot(picked[i], own[i], preferred_element_type=jnp.float32)
        total = term if total is None else total + term
    before[...] = accumulate(total, picked, 1, near, per, width)
    place_pieces(buffer, seg_id, 0, pieces, twins)


def far_kernel(per, width, first, picked, before, c2e, piece, twin, filled, out, buffer):
    place_pieces(buffer, lax.axis_index("morton"), first, [piece], [twin])
    total = before[...]
    for k in range(buffer.shape[0]):
        total = accumulate(total, picked, k + 2, buffer.at[k], per, width)
    check = total.astype(jnp.bfloat16)
    out[...] = jnp.dot(check, c2e[...], preferred_element_type=jnp.float32).T


def per_device(multipoles, counts, sources, relpos, operators, c2e):
    segs, lanes = lax.axis_size("morton"), lax.axis_size("lane")
    boxes, width = multipoles.shape[1:]
    per = operators.shape[0]
    rows = per * width

    block = multipoles[0].T
    flat = operators.reshape(rows, width)
    eighth, quarter = part_rows(rows, segs), part_rows(rows, 2)
    vmem = pl.BlockSpec(memory_space=pltpu.VMEM)
    hbm = pl.BlockSpec(memory_space=pltpu.HBM)

    def call(kernel, out, args, specs=None, scratch=(), flops=0, limit=24 << 20, alias=None):
        return pl.pallas_call(
            kernel,
            out_shape=out,
            in_specs=specs or [vmem] * len(args),
            out_specs=jax.tree.map(lambda _: vmem, out),
            scratch_shapes=list(scratch),
            input_output_aliases=alias or {},
            compiler_params=pltpu.CompilerParams(vmem_limit_bytes=limit),
            cost_estimate=pl.CostEstimate(flops=flops, bytes_accessed=1 << 20, transcendentals=0),
        )(*args)

    small, mid, block_near = call(
        prep_kernel,
        (
            jax.ShapeDtypeStruct((1, eighth, width), operators.dtype),
            jax.ShapeDtypeStruct((1, quarter, width), operators.dtype),
            jax.ShapeDtypeStruct(block.shape, block.dtype),
        ),
        (pltpu.with_memory_space_constraint(flat, pltpu.HBM), pltpu.with_memory_space_constraint(block, pltpu.HBM)),
        specs=[hbm, hbm],
        scratch=[pltpu.SemaphoreType.DMA((3,))],
    )
    twin = lax.ppermute(block, "morton", pairs_xor(segs, 1))
    other = lax.ppermute(block, "morton", pairs_odd(segs))
    column = jnp.concatenate([block_near, twin, other], axis=0)
    near = lax.ppermute(column, "lane", pairs_xor(lanes, 1))
    far = lax.ppermute(column, ("morton", "lane"), pairs_far(segs, lanes))
    landed = [lax.ppermute(small, "lane", pairs_xor(lanes, k)) for k in range(2, lanes)]
    close = lax.ppermute(mid, "lane", pairs_xor(lanes, 1))

    landed = jnp.concatenate(landed, axis=0)
    pieces = [landed]
    while len(pieces) < segs // 2:
        step = len(pieces)
        pieces += [lax.ppermute(piece, "morton", pairs_xor(segs, 2 * step)) for piece in pieces]
    close_twin = lax.ppermute(close, "morton", pairs_xor(segs, 1))
    twins = [lax.ppermute(piece, "morton", pairs_xor(segs, 1)) for piece in pieces]

    sums = jax.ShapeDtypeStruct((boxes, width), jnp.float32)
    total = lanes * per
    part, index, c2e_near = call(
        functools.partial(first_kernel, boxes, per, lanes),
        (
            jax.ShapeDtypeStruct((total, width, boxes), jnp.bfloat16),
            jax.ShapeDtypeStruct((total, boxes), jnp.int32),
            jax.ShapeDtypeStruct(c2e.shape, c2e.dtype),
        ),
        (counts, jnp.transpose(sources, (2, 0, 1)), jnp.transpose(relpos, (2, 0, 1)), column, c2e),
        flops=2 * total * boxes * boxes * 3 * width,
    )
    picked = call(
        functools.partial(second_kernel, boxes),
        jax.ShapeDtypeStruct((total, boxes, width), jnp.bfloat16),
        (index, part, near, far),
        specs=[vmem] * 4,
        flops=2 * total * boxes * boxes * 6 * width,
    )
    buffer = jax.ShapeDtypeStruct((lanes - 2, eighth * segs, width), jnp.bfloat16)
    early = len(pieces) - 1
    before, buffer_mid = call(
        functools.partial(mid_kernel, per, width, early),
        (sums, buffer),
        (picked, operators, close, close_twin, *pieces[:early], *twins[:early]),
        scratch=[pltpu.VMEM((2 * quarter, width), jnp.bfloat16)],
        flops=4 * boxes * rows * width,
    )
    density, _ = call(
        functools.partial(far_kernel, per, width, early),
        (jax.ShapeDtypeStruct((width, boxes), jnp.float32), buffer),
        (picked, before, c2e_near, pieces[early], twins[early], buffer_mid),
        alias={5: 1},
        flops=2 * lanes * boxes * rows * width,
    )
    return density.T.reshape(1, boxes, width)


def solution(mesh):
    return jax.shard_map(
        per_device,
        mesh=mesh,
        in_specs=(
            P("morton", "lane", None),
            P("morton", "lane"),
            P("morton", "lane", None),
            P("morton", "lane", None),
            P("lane", None, None),
            P(),
        ),
        out_specs=P("morton", "lane", None),
        check_vma=False,
    )
```

```python
import functools

import jax
import jax.numpy as jnp
from jax import lax
from jax.experimental import pallas as pl
from jax.experimental.pallas import tpu as pltpu
from jax.sharding import PartitionSpec as P


def pairs_xor(count, mask):
    return [(i, i ^ mask) for i in range(count)]


def pairs_odd(count):
    out = [(0, count - 1), (count - 1, 0)]
    for i in range(1, count - 1, 2):
        out += [(i, i + 1), (i + 1, i)]
    return out


def pairs_far(segs, lanes):
    ends = (0, lanes - 1)
    out = [(i * lanes + j, (i ^ 1) * lanes + j) for i in range(segs) for j in ends]
    for i, j in pairs_odd(lanes):
        if i not in ends:
            out += [(k * lanes + i, k * lanes + j) for k in range(segs)]
    return out


def part_rows(rows, parts):
    return 16 * -(-rows // (16 * parts))


def copy_part(flat, out, size, index, sem, act):
    rows = flat.shape[0]
    whole, rest = divmod(rows, size)

    def move(count):
        start = pl.multiple_of(index * size, 16)
        copy = pltpu.make_async_copy(flat.at[pl.ds(start, count), :], out.at[pl.ds(0, count), :], sem)
        copy.start() if act == "start" else copy.wait()

    pl.when(index < whole)(lambda: move(size))
    if rest:
        pl.when(index == whole)(lambda: move(rest))


def packing(width, size):
    full = width // 128
    tail = width - 128 * full
    fold = 128 // tail if tail else 1
    third = 16 * -(-size // (16 * fold)) if tail else 0
    return full, tail, fold, third


def packed_rows(width, size):
    full, _, _, third = packing(width, size)
    return full * size + third


def pack(out, part):
    size, width = part.shape
    full, tail, fold, third = packing(width, size)
    for t in range(full):
        out[t * size : (t + 1) * size, :] = part[:, t * 128 : (t + 1) * 128]
    if not tail:
        return
    columns = []
    for f in range(fold):
        count = max(0, min(size - f * third, third))
        column = []
        if count:
            column.append(part[f * third : f * third + count, 128 * full :])
        if count < third:
            column.append(jnp.zeros((third - count, tail), part.dtype))
        columns.append(jnp.concatenate(column, axis=0) if len(column) > 1 else column[0])
    if fold * tail < 128:
        columns.append(jnp.zeros((third, 128 - fold * tail), part.dtype))
    out[full * size :, :] = jnp.concatenate(columns, axis=1)


def place_part(buffer, index, part, size):
    full, tail, fold, third = packing(buffer.shape[1], size)
    at = pl.multiple_of(index * size, 16)
    for t in range(full):
        buffer[pl.ds(at, size), t * 128 : (t + 1) * 128] = part[t * size : (t + 1) * size, :]
    for f in range(fold if tail else 0):
        count = min(size - f * third, third)
        if count > 0:
            spot = pl.ds(pl.multiple_of(at + f * third, 16), count)
            buffer[spot, 128 * full :] = part[full * size : full * size + count, f * tail : (f + 1) * tail]


def prep_kernel(flat, block, small, mid, block_out, small_raw, mid_raw, sems):
    seg_id = lax.axis_index("morton")
    jobs = ((small_raw, seg_id, sems.at[0]), (mid_raw, seg_id % 2, sems.at[1]))
    whole = pltpu.make_async_copy(block, block_out, sems.at[2])
    for raw, index, sem in jobs:
        copy_part(flat, raw, raw.shape[0], index, sem, "start")
    whole.start()
    for (raw, index, sem), out in zip(jobs, (small, mid)):
        copy_part(flat, raw, raw.shape[0], index, sem, "wait")
        pack(out.at[0], raw[...])
    whole.wait()


def side_tables(refs, width):
    parts = []
    for ref in refs:
        for j in range(3):
            parts.append(ref[pl.ds(j * width, width), :])
    return jnp.concatenate(parts, axis=1)


def pick_rows(index, table, first, at, count, boxes):
    spot = lax.broadcasted_iota(jnp.int32, (table.shape[1], boxes), 0) + first
    picks = [(index[at + i : at + i + 1, :] == spot).astype(jnp.float32).astype(jnp.bfloat16) for i in range(count)]
    picks = jnp.concatenate(picks, axis=1) if count > 1 else picks[0]
    return jnp.dot(table, picks, preferred_element_type=jnp.float32).astype(jnp.bfloat16)


def first_kernel(boxes, per, lanes, counts, sources, relpos, column, c2e, out, index_out, c2e_out):
    lane_id, seg_id = lax.axis_index("lane"), lax.axis_index("morton")
    code = sources[:, 0, :]
    rel = relpos[:, 0, :]
    slot = lax.broadcasted_iota(jnp.int32, rel.shape, 0)
    live = slot < counts[...]
    nb = jnp.zeros_like(code)
    for k in range(1, 9):
        nb = nb + (code >= k * boxes).astype(jnp.int32)
    a = (nb >= 3).astype(jnp.int32) + (nb >= 6).astype(jnp.int32)
    b = nb - 3 * a
    offset = code - nb * boxes

    def place(v, odd):
        return jnp.where(v == 1, 0, jnp.where(v == 2 - 2 * odd, 1, 2))

    mapped = (place(b, lane_id % 2) * 3 + place(a, seg_id % 2)) * boxes + offset + 1
    mapped = jnp.where(live, mapped, 0)
    rows = []
    for g in range(lanes):
        for i in range(per):
            wanted = (lane_id ^ g) * per + i
            rows.append(jnp.sum(jnp.where(rel == wanted, mapped, 0), axis=0, keepdims=True) - 1)
    index = jnp.concatenate(rows, axis=0)
    index_out[...] = index
    table = side_tables((column,), out.shape[1])
    for at in range(0, len(rows), 2):
        count = min(2, len(rows) - at)
        found = pick_rows(index, table, 0, at, count, boxes)
        for i in range(count):
            out[at + i] = found[:, i * boxes : (i + 1) * boxes]
    c2e_out[...] = c2e[...]


def second_kernel(boxes, index, part, near, far, out):
    table = side_tables((near, far), out.shape[2])
    values = index[...]
    total = values.shape[0]
    for at in range(0, total, 2):
        count = min(2, total - at)
        found = pick_rows(values, table, 3 * boxes, at, count, boxes)
        for i in range(count):
            out[at + i] = (part[at + i] + found[:, i * boxes : (i + 1) * boxes]).T


def accumulate(total, picked, group, buffer, per, width):
    for i in range(per):
        term = jnp.dot(picked[group * per + i], buffer[pl.ds(i * width, width), :], preferred_element_type=jnp.float32)
        total = total + term
    return total


def place_pieces(buffer, seg_id, first, pieces, twins, size):
    for k in range(pieces[0].shape[0]):
        for j, (piece, twin) in enumerate(zip(pieces, twins)):
            place_part(buffer.at[k], seg_id ^ (2 * (first + j)), piece[k], size)
            place_part(buffer.at[k], seg_id ^ (2 * (first + j) + 1), twin[k], size)


def mid_kernel(per, width, count, quarter, eighth, picked, own, close, close_twin, *refs):
    pieces, twins = refs[:count], refs[count : 2 * count]
    before, buffer, near = refs[2 * count :]
    seg_id = lax.axis_index("morton")
    core = seg_id % 2
    place_part(near, core, close[0], quarter)
    place_part(near, 1 - core, close_twin[0], quarter)
    total = None
    for i in range(per):
        term = jnp.dot(picked[i], own[i], preferred_element_type=jnp.float32)
        total = term if total is None else total + term
    before[...] = accumulate(total, picked, 1, near, per, width)
    place_pieces(buffer, seg_id, 0, pieces, twins, eighth)


def far_kernel(per, width, first, eighth, picked, before, c2e, piece, twin, filled, out, buffer):
    place_pieces(buffer, lax.axis_index("morton"), first, [piece], [twin], eighth)
    total = before[...]
    for k in range(buffer.shape[0]):
        total = accumulate(total, picked, k + 2, buffer.at[k], per, width)
    check = total.astype(jnp.bfloat16)
    out[...] = jnp.dot(check, c2e[...], preferred_element_type=jnp.float32).T


def per_device(multipoles, counts, sources, relpos, operators, c2e):
    segs, lanes = lax.axis_size("morton"), lax.axis_size("lane")
    boxes, width = multipoles.shape[1:]
    per = operators.shape[0]
    rows = per * width

    block = multipoles[0].T
    flat = operators.reshape(rows, width)
    eighth, quarter = part_rows(rows, segs), part_rows(rows, 2)
    vmem = pl.BlockSpec(memory_space=pltpu.VMEM)
    hbm = pl.BlockSpec(memory_space=pltpu.HBM)

    def call(kernel, out, args, specs=None, scratch=(), flops=0, limit=24 << 20, alias=None):
        return pl.pallas_call(
            kernel,
            out_shape=out,
            in_specs=specs or [vmem] * len(args),
            out_specs=jax.tree.map(lambda _: vmem, out),
            scratch_shapes=list(scratch),
            input_output_aliases=alias or {},
            compiler_params=pltpu.CompilerParams(vmem_limit_bytes=limit),
            cost_estimate=pl.CostEstimate(flops=flops, bytes_accessed=1 << 20, transcendentals=0),
        )(*args)

    small, mid, block_near = call(
        prep_kernel,
        (
            jax.ShapeDtypeStruct((1, packed_rows(width, eighth), 128), operators.dtype),
            jax.ShapeDtypeStruct((1, packed_rows(width, quarter), 128), operators.dtype),
            jax.ShapeDtypeStruct(block.shape, block.dtype),
        ),
        (pltpu.with_memory_space_constraint(flat, pltpu.HBM), pltpu.with_memory_space_constraint(block, pltpu.HBM)),
        specs=[hbm, hbm],
        scratch=[
            pltpu.VMEM((eighth, width), operators.dtype),
            pltpu.VMEM((quarter, width), operators.dtype),
            pltpu.SemaphoreType.DMA((3,)),
        ],
    )
    twin = lax.ppermute(block, "morton", pairs_xor(segs, 1))
    other = lax.ppermute(block, "morton", pairs_odd(segs))
    column = jnp.concatenate([block_near, twin, other], axis=0)
    near = lax.ppermute(column, "lane", pairs_xor(lanes, 1))
    far = lax.ppermute(column, ("morton", "lane"), pairs_far(segs, lanes))
    landed = [lax.ppermute(small, "lane", pairs_xor(lanes, k)) for k in range(2, lanes)]
    close = lax.ppermute(mid, "lane", pairs_xor(lanes, 1))

    landed = jnp.concatenate(landed, axis=0)
    pieces = [landed]
    while len(pieces) < segs // 2:
        step = len(pieces)
        pieces += [lax.ppermute(piece, "morton", pairs_xor(segs, 2 * step)) for piece in pieces]
    close_twin = lax.ppermute(close, "morton", pairs_xor(segs, 1))
    twins = [lax.ppermute(piece, "morton", pairs_xor(segs, 1)) for piece in pieces]

    sums = jax.ShapeDtypeStruct((boxes, width), jnp.float32)
    total = lanes * per
    part, index, c2e_near = call(
        functools.partial(first_kernel, boxes, per, lanes),
        (
            jax.ShapeDtypeStruct((total, width, boxes), jnp.bfloat16),
            jax.ShapeDtypeStruct((total, boxes), jnp.int32),
            jax.ShapeDtypeStruct(c2e.shape, c2e.dtype),
        ),
        (counts, jnp.transpose(sources, (2, 0, 1)), jnp.transpose(relpos, (2, 0, 1)), column, c2e),
        flops=2 * total * boxes * boxes * 3 * width,
    )
    picked = call(
        functools.partial(second_kernel, boxes),
        jax.ShapeDtypeStruct((total, boxes, width), jnp.bfloat16),
        (index, part, near, far),
        specs=[vmem] * 4,
        flops=2 * total * boxes * boxes * 6 * width,
    )
    buffer = jax.ShapeDtypeStruct((lanes - 2, eighth * segs, width), jnp.bfloat16)
    early = len(pieces) - 1
    before, buffer_mid = call(
        functools.partial(mid_kernel, per, width, early, quarter, eighth),
        (sums, buffer),
        (picked, operators, close, close_twin, *pieces[:early], *twins[:early]),
        scratch=[pltpu.VMEM((2 * quarter, width), jnp.bfloat16)],
        flops=4 * boxes * rows * width,
    )
    density, _ = call(
        functools.partial(far_kernel, per, width, early, eighth),
        (jax.ShapeDtypeStruct((width, boxes), jnp.float32), buffer),
        (picked, before, c2e_near, pieces[early], twins[early], buffer_mid),
        alias={5: 1},
        flops=2 * lanes * boxes * rows * width,
    )
    return density.T.reshape(1, boxes, width)


def solution(mesh):
    return jax.shard_map(
        per_device,
        mesh=mesh,
        in_specs=(
            P("morton", "lane", None),
            P("morton", "lane"),
            P("morton", "lane", None),
            P("morton", "lane", None),
            P("lane", None, None),
            P(),
        ),
        out_specs=P("morton", "lane", None),
        check_vma=False,
    )
```

```python
import functools

import jax
import jax.numpy as jnp
from jax import lax
from jax.experimental import pallas as pl
from jax.experimental.pallas import tpu as pltpu
from jax.sharding import PartitionSpec as P


def pairs_xor(count, mask):
    return [(i, i ^ mask) for i in range(count)]


def pairs_odd(count):
    out = [(0, count - 1), (count - 1, 0)]
    for i in range(1, count - 1, 2):
        out += [(i, i + 1), (i + 1, i)]
    return out


def pairs_far(segs, lanes):
    ends = (0, lanes - 1)
    out = [(i * lanes + j, (i ^ 1) * lanes + j) for i in range(segs) for j in ends]
    for i, j in pairs_odd(lanes):
        if i not in ends:
            out += [(k * lanes + i, k * lanes + j) for k in range(segs)]
    return out


def part_rows(rows, parts):
    return 16 * -(-rows // (16 * parts))


def copy_part(flat, out, size, index, sem, act):
    rows = flat.shape[0]
    whole, rest = divmod(rows, size)

    def move(count):
        start = pl.multiple_of(index * size, 16)
        copy = pltpu.make_async_copy(flat.at[pl.ds(start, count), :], out.at[pl.ds(0, count), :], sem)
        copy.start() if act == "start" else copy.wait()

    pl.when(index < whole)(lambda: move(size))
    if rest:
        pl.when(index == whole)(lambda: move(rest))


def packing(width, size):
    full = width // 128
    tail = width - 128 * full
    fold = 128 // tail if tail else 1
    third = 16 * -(-size // (16 * fold)) if tail else 0
    return full, tail, fold, third


def packed_rows(width, size):
    full, _, _, third = packing(width, size)
    return full * size + third


def pack(out, part):
    size, width = part.shape
    full, tail, fold, third = packing(width, size)
    for t in range(full):
        out[t * size : (t + 1) * size, :] = part[:, t * 128 : (t + 1) * 128]
    if not tail:
        return
    columns = []
    for f in range(fold):
        count = max(0, min(size - f * third, third))
        column = []
        if count:
            column.append(part[f * third : f * third + count, 128 * full :])
        if count < third:
            column.append(jnp.zeros((third - count, tail), part.dtype))
        columns.append(jnp.concatenate(column, axis=0) if len(column) > 1 else column[0])
    if fold * tail < 128:
        columns.append(jnp.zeros((third, 128 - fold * tail), part.dtype))
    out[full * size :, :] = jnp.concatenate(columns, axis=1)


def place_part(buffer, index, part, size):
    full, tail, fold, third = packing(buffer.shape[1], size)
    at = pl.multiple_of(index * size, 16)
    for t in range(full):
        buffer[pl.ds(at, size), t * 128 : (t + 1) * 128] = part[t * size : (t + 1) * size, :]
    for f in range(fold if tail else 0):
        count = min(size - f * third, third)
        if count > 0:
            spot = pl.ds(pl.multiple_of(at + f * third, 16), count)
            buffer[spot, 128 * full :] = part[full * size : full * size + count, f * tail : (f + 1) * tail]


def prep_kernel(flat, block, small, mid, block_out, small_raw, mid_raw, sems):
    seg_id = lax.axis_index("morton")
    jobs = ((small_raw, seg_id, sems.at[0]), (mid_raw, seg_id % 2, sems.at[1]))
    whole = pltpu.make_async_copy(block, block_out, sems.at[2])
    for raw, index, sem in jobs:
        copy_part(flat, raw, raw.shape[0], index, sem, "start")
    whole.start()
    for (raw, index, sem), out in zip(jobs, (small, mid)):
        copy_part(flat, raw, raw.shape[0], index, sem, "wait")
        pack(out.at[0], raw[...])
    whole.wait()


def side_tables(refs, width):
    parts = []
    for ref in refs:
        for j in range(3):
            parts.append(ref[pl.ds(j * width, width), :])
    return jnp.concatenate(parts, axis=1)


def pick_rows(index, table, first, at, count, boxes):
    spot = lax.broadcasted_iota(jnp.int32, (table.shape[1], boxes), 0) + first
    picks = [(index[at + i : at + i + 1, :] == spot).astype(jnp.float32).astype(jnp.bfloat16) for i in range(count)]
    picks = jnp.concatenate(picks, axis=1) if count > 1 else picks[0]
    return jnp.dot(table, picks, preferred_element_type=jnp.float32).astype(jnp.bfloat16)


def first_kernel(boxes, per, lanes, counts, sources, relpos, column, c2e, out, index_out, c2e_out):
    lane_id, seg_id = lax.axis_index("lane"), lax.axis_index("morton")
    code = sources[:, 0, :]
    rel = relpos[:, 0, :]
    slot = lax.broadcasted_iota(jnp.int32, rel.shape, 0)
    live = slot < counts[...]
    nb = jnp.zeros_like(code)
    for k in range(1, 9):
        nb = nb + (code >= k * boxes).astype(jnp.int32)
    a = (nb >= 3).astype(jnp.int32) + (nb >= 6).astype(jnp.int32)
    b = nb - 3 * a
    offset = code - nb * boxes

    def place(v, odd):
        return jnp.where(v == 1, 0, jnp.where(v == 2 - 2 * odd, 1, 2))

    mapped = (place(b, lane_id % 2) * 3 + place(a, seg_id % 2)) * boxes + offset + 1
    mapped = jnp.where(live, mapped, 0)
    rows = []
    for g in range(lanes):
        for i in range(per):
            wanted = (lane_id ^ g) * per + i
            rows.append(jnp.sum(jnp.where(rel == wanted, mapped, 0), axis=0, keepdims=True) - 1)
    index = jnp.concatenate(rows, axis=0)
    index_out[...] = index
    table = side_tables((column,), out.shape[1])
    for at in range(0, len(rows), 2):
        count = min(2, len(rows) - at)
        found = pick_rows(index, table, 0, at, count, boxes)
        for i in range(count):
            out[at + i] = found[:, i * boxes : (i + 1) * boxes]
    c2e_out[...] = c2e[...]


def second_kernel(boxes, per, index, part, near, far, out, stacked):
    width = part.shape[1]
    table = side_tables((near, far), width)
    values = index[...]
    total = values.shape[0]
    for at in range(0, total, 2):
        count = min(2, total - at)
        found = pick_rows(values, table, 3 * boxes, at, count, boxes)
        for i in range(count):
            spot = slice((at + i) * width, (at + i + 1) * width)
            stacked[spot, :] = part[at + i] + found[:, i * boxes : (i + 1) * boxes]
    for g in range(total // per):
        out[g] = stacked[g * per * width : (g + 1) * per * width, :].T


def accumulate(total, picked, group, buffer):
    rows = picked.shape[2]
    return total + jnp.dot(picked[group], buffer[pl.ds(0, rows), :], preferred_element_type=jnp.float32)


def place_pieces(buffer, seg_id, first, pieces, size):
    for k in range(pieces[0].shape[0]):
        for j, piece in enumerate(pieces):
            place_part(buffer.at[k], seg_id ^ (2 * (first + j)), piece[k], size)


def mid_kernel(count, quarter, eighth, picked, own, close, close_twin, *refs):
    pieces, twins = refs[:count], refs[count : 2 * count - 1]
    before, buffer, near = refs[2 * count - 1 :]
    seg_id = lax.axis_index("morton")
    core = seg_id % 2
    place_part(near, core, close[0], quarter)
    place_part(near, 1 - core, close_twin[0], quarter)
    total = jnp.dot(picked[0], own[...], preferred_element_type=jnp.float32)
    before[...] = accumulate(total, picked, 1, near)
    place_pieces(buffer, seg_id, 0, pieces, eighth)
    place_pieces(buffer, seg_id ^ 1, 0, twins, eighth)


def far_kernel(first, eighth, picked, before, c2e, twin, filled, out, buffer):
    place_pieces(buffer, lax.axis_index("morton") ^ 1, first, [twin], eighth)
    total = before[...]
    for k in range(buffer.shape[0]):
        total = accumulate(total, picked, k + 2, buffer.at[k])
    check = total.astype(jnp.bfloat16)
    out[...] = jnp.dot(check, c2e[...], preferred_element_type=jnp.float32).T


def per_device(multipoles, counts, sources, relpos, operators, c2e):
    segs, lanes = lax.axis_size("morton"), lax.axis_size("lane")
    boxes, width = multipoles.shape[1:]
    per = operators.shape[0]
    rows = per * width

    block = multipoles[0].T
    flat = operators.reshape(rows, width)
    eighth, quarter = part_rows(rows, segs), part_rows(rows, 2)
    vmem = pl.BlockSpec(memory_space=pltpu.VMEM)
    hbm = pl.BlockSpec(memory_space=pltpu.HBM)

    def call(kernel, out, args, specs=None, scratch=(), flops=0, limit=24 << 20, alias=None):
        return pl.pallas_call(
            kernel,
            out_shape=out,
            in_specs=specs or [vmem] * len(args),
            out_specs=jax.tree.map(lambda _: vmem, out),
            scratch_shapes=list(scratch),
            input_output_aliases=alias or {},
            compiler_params=pltpu.CompilerParams(vmem_limit_bytes=limit),
            cost_estimate=pl.CostEstimate(flops=flops, bytes_accessed=1 << 20, transcendentals=0),
        )(*args)

    small, mid, block_near = call(
        prep_kernel,
        (
            jax.ShapeDtypeStruct((1, packed_rows(width, eighth), 128), operators.dtype),
            jax.ShapeDtypeStruct((1, packed_rows(width, quarter), 128), operators.dtype),
            jax.ShapeDtypeStruct(block.shape, block.dtype),
        ),
        (pltpu.with_memory_space_constraint(flat, pltpu.HBM), pltpu.with_memory_space_constraint(block, pltpu.HBM)),
        specs=[hbm, hbm],
        scratch=[
            pltpu.VMEM((eighth, width), operators.dtype),
            pltpu.VMEM((quarter, width), operators.dtype),
            pltpu.SemaphoreType.DMA((3,)),
        ],
    )
    twin = lax.ppermute(block, "morton", pairs_xor(segs, 1))
    other = lax.ppermute(block, "morton", pairs_odd(segs))
    column = jnp.concatenate([block_near, twin, other], axis=0)
    near = lax.ppermute(column, "lane", pairs_xor(lanes, 1))
    far = lax.ppermute(column, ("morton", "lane"), pairs_far(segs, lanes))
    landed = [lax.ppermute(small, "lane", pairs_xor(lanes, k)) for k in range(2, lanes)]
    close = lax.ppermute(mid, "lane", pairs_xor(lanes, 1))

    landed = jnp.concatenate(landed, axis=0)
    pieces = [landed]
    while len(pieces) < segs // 2:
        step = len(pieces)
        pieces += [lax.ppermute(piece, "morton", pairs_xor(segs, 2 * step)) for piece in pieces]
    close_twin = lax.ppermute(close, "morton", pairs_xor(segs, 1))
    twins = [lax.ppermute(piece, "morton", pairs_xor(segs, 1)) for piece in pieces]

    sums = jax.ShapeDtypeStruct((boxes, width), jnp.float32)
    total = lanes * per
    part, index, c2e_near = call(
        functools.partial(first_kernel, boxes, per, lanes),
        (
            jax.ShapeDtypeStruct((total, width, boxes), jnp.bfloat16),
            jax.ShapeDtypeStruct((total, boxes), jnp.int32),
            jax.ShapeDtypeStruct(c2e.shape, c2e.dtype),
        ),
        (counts, jnp.transpose(sources, (2, 0, 1)), jnp.transpose(relpos, (2, 0, 1)), column, c2e),
        flops=2 * total * boxes * boxes * 3 * width,
    )
    picked = call(
        functools.partial(second_kernel, boxes, per),
        jax.ShapeDtypeStruct((lanes, boxes, rows), jnp.bfloat16),
        (index, part, near, far),
        scratch=[pltpu.VMEM((total * width, boxes), jnp.bfloat16)],
        flops=2 * total * boxes * boxes * 6 * width,
    )
    buffer = jax.ShapeDtypeStruct((lanes - 2, eighth * segs, width), jnp.bfloat16)
    early = len(pieces) - 1
    before, buffer_mid = call(
        functools.partial(mid_kernel, len(pieces), quarter, eighth),
        (sums, buffer),
        (picked, flat, close, close_twin, *pieces, *twins[:early]),
        scratch=[pltpu.VMEM((2 * quarter, width), jnp.bfloat16)],
        flops=4 * boxes * rows * width,
    )
    density, _ = call(
        functools.partial(far_kernel, early, eighth),
        (jax.ShapeDtypeStruct((width, boxes), jnp.float32), buffer),
        (picked, before, c2e_near, twins[early], buffer_mid),
        alias={4: 1},
        flops=2 * lanes * boxes * rows * width,
    )
    return density.T.reshape(1, boxes, width)


def solution(mesh):
    return jax.shard_map(
        per_device,
        mesh=mesh,
        in_specs=(
            P("morton", "lane", None),
            P("morton", "lane"),
            P("morton", "lane", None),
            P("morton", "lane", None),
            P("lane", None, None),
            P(),
        ),
        out_specs=P("morton", "lane", None),
        check_vma=False,
    )
```

```python
import functools

import jax
import jax.numpy as jnp
from jax import lax
from jax.experimental import pallas as pl
from jax.experimental.pallas import tpu as pltpu
from jax.sharding import PartitionSpec as P


def pairs_xor(count, mask):
    return [(i, i ^ mask) for i in range(count)]


def pairs_odd(count):
    out = [(0, count - 1), (count - 1, 0)]
    for i in range(1, count - 1, 2):
        out += [(i, i + 1), (i + 1, i)]
    return out


def pairs_far(segs, lanes):
    ends = (0, lanes - 1)
    out = [(i * lanes + j, (i ^ 1) * lanes + j) for i in range(segs) for j in ends]
    for i, j in pairs_odd(lanes):
        if i not in ends:
            out += [(k * lanes + i, k * lanes + j) for k in range(segs)]
    return out


def part_rows(rows, parts):
    return 16 * -(-rows // (16 * parts))


def copy_part(flat, out, size, index, sem, act):
    rows = flat.shape[0]
    whole, rest = divmod(rows, size)

    def move(count):
        start = pl.multiple_of(index * size, 16)
        copy = pltpu.make_async_copy(flat.at[pl.ds(start, count), :], out.at[pl.ds(0, count), :], sem)
        copy.start() if act == "start" else copy.wait()

    pl.when(index < whole)(lambda: move(size))
    if rest:
        pl.when(index == whole)(lambda: move(rest))


def packing(width, size):
    full = width // 128
    tail = width - 128 * full
    fold = 128 // tail if tail else 1
    third = 16 * -(-size // (16 * fold)) if tail else 0
    return full, tail, fold, third


def packed_rows(width, size):
    full, _, _, third = packing(width, size)
    return full * size + third


def pack(out, part):
    size, width = part.shape
    full, tail, fold, third = packing(width, size)
    for t in range(full):
        out[t * size : (t + 1) * size, :] = part[:, t * 128 : (t + 1) * 128]
    if not tail:
        return
    columns = []
    for f in range(fold):
        count = max(0, min(size - f * third, third))
        column = []
        if count:
            column.append(part[f * third : f * third + count, 128 * full :])
        if count < third:
            column.append(jnp.zeros((third - count, tail), part.dtype))
        columns.append(jnp.concatenate(column, axis=0) if len(column) > 1 else column[0])
    if fold * tail < 128:
        columns.append(jnp.zeros((third, 128 - fold * tail), part.dtype))
    out[full * size :, :] = jnp.concatenate(columns, axis=1)


def place_part(buffer, index, part, size):
    full, tail, fold, third = packing(buffer.shape[1], size)
    at = pl.multiple_of(index * size, 16)
    for t in range(full):
        buffer[pl.ds(at, size), t * 128 : (t + 1) * 128] = part[t * size : (t + 1) * size, :]
    for f in range(fold if tail else 0):
        count = min(size - f * third, third)
        if count > 0:
            spot = pl.ds(pl.multiple_of(at + f * third, 16), count)
            buffer[spot, 128 * full :] = part[full * size : full * size + count, f * tail : (f + 1) * tail]


def prep_kernel(flat, block, small, flat_out, block_out, raw, sems):
    seg_id = lax.axis_index("morton")
    wholes = [pltpu.make_async_copy(flat, flat_out, sems.at[1]), pltpu.make_async_copy(block, block_out, sems.at[2])]
    copy_part(flat, raw, raw.shape[0], seg_id, sems.at[0], "start")
    for whole in wholes:
        whole.start()
    copy_part(flat, raw, raw.shape[0], seg_id, sems.at[0], "wait")
    pack(small.at[0], raw[...])
    for whole in wholes:
        whole.wait()


def half_kernel(size, flat, mid):
    rows = flat.shape[0]

    def move(start, count):
        part = flat[start : start + count, :]
        if count < size:
            part = jnp.concatenate([part, jnp.zeros((size - count, flat.shape[1]), flat.dtype)], axis=0)
        pack(mid.at[0], part)

    core = lax.axis_index("morton") % 2
    pl.when(core == 0)(lambda: move(0, size))
    pl.when(core == 1)(lambda: move(size, rows - size))


def side_tables(refs, width):
    parts = []
    for ref in refs:
        for j in range(3):
            parts.append(ref[pl.ds(j * width, width), :])
    return jnp.concatenate(parts, axis=1)


def pick_rows(index, table, first, at, count, boxes):
    spot = lax.broadcasted_iota(jnp.int32, (table.shape[1], boxes), 0) + first
    picks = [(index[at + i : at + i + 1, :] == spot).astype(jnp.float32).astype(jnp.bfloat16) for i in range(count)]
    picks = jnp.concatenate(picks, axis=1) if count > 1 else picks[0]
    return jnp.dot(table, picks, preferred_element_type=jnp.float32).astype(jnp.bfloat16)


def first_kernel(boxes, per, lanes, counts, sources, relpos, column, c2e, out, index_out, c2e_out):
    lane_id, seg_id = lax.axis_index("lane"), lax.axis_index("morton")
    code = sources[:, 0, :]
    rel = relpos[:, 0, :]
    slot = lax.broadcasted_iota(jnp.int32, rel.shape, 0)
    live = slot < counts[...]
    nb = jnp.zeros_like(code)
    for k in range(1, 9):
        nb = nb + (code >= k * boxes).astype(jnp.int32)
    a = (nb >= 3).astype(jnp.int32) + (nb >= 6).astype(jnp.int32)
    b = nb - 3 * a
    offset = code - nb * boxes

    def place(v, odd):
        return jnp.where(v == 1, 0, jnp.where(v == 2 - 2 * odd, 1, 2))

    mapped = (place(b, lane_id % 2) * 3 + place(a, seg_id % 2)) * boxes + offset + 1
    mapped = jnp.where(live, mapped, 0)
    rows = []
    for g in range(lanes):
        for i in range(per):
            wanted = (lane_id ^ g) * per + i
            rows.append(jnp.sum(jnp.where(rel == wanted, mapped, 0), axis=0, keepdims=True) - 1)
    index = jnp.concatenate(rows, axis=0)
    index_out[...] = index
    table = side_tables((column,), out.shape[1])
    for at in range(0, len(rows), 2):
        count = min(2, len(rows) - at)
        found = pick_rows(index, table, 0, at, count, boxes)
        for i in range(count):
            out[at + i] = found[:, i * boxes : (i + 1) * boxes]
    c2e_out[...] = c2e[...]


def second_kernel(boxes, per, index, part, near, far, out, stacked):
    width = part.shape[1]
    table = side_tables((near, far), width)
    values = index[...]
    total = values.shape[0]
    for at in range(0, total, 2):
        count = min(2, total - at)
        found = pick_rows(values, table, 3 * boxes, at, count, boxes)
        for i in range(count):
            spot = slice((at + i) * width, (at + i + 1) * width)
            stacked[spot, :] = part[at + i] + found[:, i * boxes : (i + 1) * boxes]
    for g in range(total // per):
        out[g] = stacked[g * per * width : (g + 1) * per * width, :].T


def accumulate(total, picked, group, buffer):
    rows = picked.shape[2]
    return total + jnp.dot(picked[group], buffer[pl.ds(0, rows), :], preferred_element_type=jnp.float32)


def place_pieces(buffer, seg_id, first, pieces, size):
    for k in range(pieces[0].shape[0]):
        for j, piece in enumerate(pieces):
            place_part(buffer.at[k], seg_id ^ (2 * (first + j)), piece[k], size)


def mid_kernel(count, quarter, eighth, picked, own, close, close_twin, *refs):
    pieces, twins = refs[:count], refs[count : 2 * count - 1]
    before, buffer, near = refs[2 * count - 1 :]
    seg_id = lax.axis_index("morton")
    core = seg_id % 2
    place_part(near, core, close[0], quarter)
    place_part(near, 1 - core, close_twin[0], quarter)
    total = jnp.dot(picked[0], own[...], preferred_element_type=jnp.float32)
    before[...] = accumulate(total, picked, 1, near)
    place_pieces(buffer, seg_id, 0, pieces, eighth)
    place_pieces(buffer, seg_id ^ 1, 0, twins, eighth)


def far_kernel(first, eighth, picked, before, c2e, twin, filled, out, buffer):
    place_pieces(buffer, lax.axis_index("morton") ^ 1, first, [twin], eighth)
    total = before[...]
    for k in range(buffer.shape[0]):
        total = accumulate(total, picked, k + 2, buffer.at[k])
    check = total.astype(jnp.bfloat16)
    out[...] = jnp.dot(check, c2e[...], preferred_element_type=jnp.float32).T


def per_device(multipoles, counts, sources, relpos, operators, c2e):
    segs, lanes = lax.axis_size("morton"), lax.axis_size("lane")
    boxes, width = multipoles.shape[1:]
    per = operators.shape[0]
    rows = per * width

    block = multipoles[0].T
    flat = operators.reshape(rows, width)
    eighth, quarter = part_rows(rows, segs), part_rows(rows, 2)
    vmem = pl.BlockSpec(memory_space=pltpu.VMEM)
    hbm = pl.BlockSpec(memory_space=pltpu.HBM)

    def call(kernel, out, args, specs=None, scratch=(), flops=0, limit=24 << 20, alias=None):
        return pl.pallas_call(
            kernel,
            out_shape=out,
            in_specs=specs or [vmem] * len(args),
            out_specs=jax.tree.map(lambda _: vmem, out),
            scratch_shapes=list(scratch),
            input_output_aliases=alias or {},
            compiler_params=pltpu.CompilerParams(vmem_limit_bytes=limit),
            cost_estimate=pl.CostEstimate(flops=flops, bytes_accessed=1 << 20, transcendentals=0),
        )(*args)

    small, flat_near, block_near = call(
        prep_kernel,
        (
            jax.ShapeDtypeStruct((1, packed_rows(width, eighth), 128), operators.dtype),
            jax.ShapeDtypeStruct(flat.shape, flat.dtype),
            jax.ShapeDtypeStruct(block.shape, block.dtype),
        ),
        [pltpu.with_memory_space_constraint(x, pltpu.HBM) for x in (flat, block)],
        specs=[hbm] * 2,
        scratch=[pltpu.VMEM((eighth, width), operators.dtype), pltpu.SemaphoreType.DMA((3,))],
    )
    mid = call(
        functools.partial(half_kernel, quarter),
        jax.ShapeDtypeStruct((1, packed_rows(width, quarter), 128), operators.dtype),
        (flat_near,),
    )
    twin = lax.ppermute(block, "morton", pairs_xor(segs, 1))
    other = lax.ppermute(block, "morton", pairs_odd(segs))
    column = jnp.concatenate([block_near, twin, other], axis=0)
    near = lax.ppermute(column, "lane", pairs_xor(lanes, 1))
    far = lax.ppermute(column, ("morton", "lane"), pairs_far(segs, lanes))
    landed = [lax.ppermute(small, "lane", pairs_xor(lanes, k)) for k in range(2, lanes)]
    close = lax.ppermute(mid, "lane", pairs_xor(lanes, 1))

    landed = jnp.concatenate(landed, axis=0)
    found = {0: landed}
    step = segs // 4
    while step:
        for j, piece in list(found.items()):
            found[j + step] = lax.ppermute(piece, "morton", pairs_xor(segs, 2 * step))
        step //= 2
    pieces = [found[j] for j in range(segs // 2)]
    close_twin = lax.ppermute(close, "morton", pairs_xor(segs, 1))
    twins = [lax.ppermute(piece, "morton", pairs_xor(segs, 1)) for piece in pieces]

    sums = jax.ShapeDtypeStruct((boxes, width), jnp.float32)
    total = lanes * per
    part, index, c2e_near = call(
        functools.partial(first_kernel, boxes, per, lanes),
        (
            jax.ShapeDtypeStruct((total, width, boxes), jnp.bfloat16),
            jax.ShapeDtypeStruct((total, boxes), jnp.int32),
            jax.ShapeDtypeStruct(c2e.shape, c2e.dtype),
        ),
        (counts, jnp.transpose(sources, (2, 0, 1)), jnp.transpose(relpos, (2, 0, 1)), column, c2e),
        flops=2 * total * boxes * boxes * 3 * width,
    )
    picked = call(
        functools.partial(second_kernel, boxes, per),
        jax.ShapeDtypeStruct((lanes, boxes, rows), jnp.bfloat16),
        (index, part, near, far),
        scratch=[pltpu.VMEM((total * width, boxes), jnp.bfloat16)],
        flops=2 * total * boxes * boxes * 6 * width,
    )
    buffer = jax.ShapeDtypeStruct((lanes - 2, eighth * segs, width), jnp.bfloat16)
    early = len(pieces) - 1
    before, buffer_mid = call(
        functools.partial(mid_kernel, len(pieces), quarter, eighth),
        (sums, buffer),
        (picked, flat_near, close, close_twin, *pieces, *twins[:early]),
        scratch=[pltpu.VMEM((2 * quarter, width), jnp.bfloat16)],
        flops=4 * boxes * rows * width,
    )
    density, _ = call(
        functools.partial(far_kernel, early, eighth),
        (jax.ShapeDtypeStruct((width, boxes), jnp.float32), buffer),
        (picked, before, c2e_near, twins[early], buffer_mid),
        alias={4: 1},
        flops=2 * lanes * boxes * rows * width,
    )
    return density.T.reshape(1, boxes, width)


def solution(mesh):
    return jax.shard_map(
        per_device,
        mesh=mesh,
        in_specs=(
            P("morton", "lane", None),
            P("morton", "lane"),
            P("morton", "lane", None),
            P("morton", "lane", None),
            P("lane", None, None),
            P(),
        ),
        out_specs=P("morton", "lane", None),
        check_vma=False,
    )
```
